32 devices in a mesh: fsdp: 32 (over z, y, x, core).
Axes of the slice: x: 2, y: 2, z: 4, core: 2. Of those that a mesh axis runs over, the one named last changes fastest.
Arguments:
- hidden_in: bfloat16 [4096, 960], P('fsdp'), may hold values from -6 to 6
- positions: int32 [4096], P('fsdp'), may hold values from 0 to 511, as said below
- norm1_gain: float32 [960], replicated, may hold values from 0.5 to 1.5
- q_weight: bfloat16 [921600], P('fsdp'), may hold values from -0.19364917 to 0.19364917
- k_weight: bfloat16 [307200], P('fsdp'), may hold values from -0.19364917 to 0.19364917
- v_weight: bfloat16 [307200], P('fsdp'), may hold values from -0.1875 to 0.1875
- o_weight: bfloat16 [921600], P('fsdp'), may hold values from -2 to 2
- norm2_gain: float32 [960], replicated, may hold values from 0.5 to 1.5
- gate_weight: bfloat16 [2457600], P('fsdp'), may hold values from -0.1875 to 0.1875
- up_weight: bfloat16 [2457600], P('fsdp'), may hold values from -0.1875 to 0.1875
- down_weight: bfloat16 [2457600], P('fsdp'), may hold values from -0.25 to 0.25
- cotangent: bfloat16 [4096, 960], P('fsdp'), may hold values from -6 to 6
Outputs:
- block_out: bfloat16 [4096, 960], P('fsdp')
- grad_in: bfloat16 [4096, 960], P('fsdp')
- grad_norm1_gain: float32 [960], replicated
- grad_q_weight: float32 [921600], P('fsdp')
- grad_k_weight: float32 [307200], P('fsdp')
- grad_v_weight: float32 [307200], P('fsdp')
- grad_o_weight: float32 [921600], P('fsdp')
- grad_norm2_gain: float32 [960], replicated
- grad_gate_weight: float32 [2457600], P('fsdp')
- grad_up_weight: float32 [2457600], P('fsdp')
- grad_down_weight: float32 [2457600], P('fsdp')
The draws below stay inside these ranges and needn't reach their ends.
Inputs may be any that keep to these rules, and one draw needn't show every extreme that they name: positions[0] is 0, and each later token's position is 0 (a new sequence starts) or one more than the previous token's. Sequences are 256 to 512 tokens long, one of them exactly 512; the last one may be cut by the end of the pack.
All inputs are finite; a program needn't handle non-finite values.
Results may differ from the reference program's by a relative error of at most 0.015.
The reference program's roundings to bfloat16 on the way count: a program that leaves them out, or rounds other values in their place, can miss the bound.
Values may be sent and summed in bfloat16 or wider, within the bound.
No kernel may reach another device: no remote copies, remote signals or barrier semaphores. Data moves between devices by JAX's collectives and lax.ppermute only.
A program may use at most 192 MiB of HBM per device.

```python
import math
import jax
import jax.numpy as jnp
from jax import lax

D = 960
KV_HEADS = 5
HEAD_DIM = 64
FF = 2560
TOK_DEV = 128
MAXLEN = 512
QW = 960
KW = 320
GROUP = 3
SPAN = 4
TOKENS = 4096


def draw_positions(key, part):
    seq_count = TOKENS // (MAXLEN // 2) + 2
    lengths = jax.random.randint(key, (seq_count,), MAXLEN // 2, MAXLEN + 1).astype(jnp.int32)
    chosen = jax.random.randint(jax.random.fold_in(key, 7), (), 0, max(seq_count // 4, 1)).astype(jnp.int32)
    lengths = jnp.where(jnp.arange(seq_count, dtype=jnp.int32) == chosen, MAXLEN, lengths).astype(jnp.int32)
    starts = (jnp.cumsum(lengths) - lengths).astype(jnp.int32)
    token_index = jnp.arange(TOKENS, dtype=jnp.int32)
    owner = jnp.sum((starts[None, :] <= token_index[:, None]).astype(jnp.int32), axis=1) - 1
    start_of = jnp.sum(jnp.where(jnp.arange(seq_count, dtype=jnp.int32)[None, :] == owner[:, None], starts[None, :], 0), axis=1)
    return (token_index - start_of).astype(jnp.int32)


def projection_draw(key, columns, salt):
    noise_key = jax.random.fold_in(key, salt)
    weight = jax.random.truncated_normal(noise_key, -6.0, 6.0, (D, columns), jnp.float32) / math.sqrt(D)
    return weight.reshape(-1).astype(jnp.bfloat16)


def draw_q_weight(key, part):
    return projection_draw(key, QW, 11)


def draw_k_weight(key, part):
    return projection_draw(key, KW, 12)


def draw_hidden_in(key, part):
    noise_key = jax.random.fold_in(key, 21)
    rows = jax.random.truncated_normal(noise_key, -6.0, 6.0, (TOKENS, D), jnp.float32)
    return rows.astype(jnp.bfloat16)


def levels(rng, extent, shards, least, top_value):
    def one(dim, shards_of):
        draws = jax.random.uniform(jax.random.fold_in(jax.random.fold_in(rng, 6), dim), (shards_of,), jnp.float32, least / len(shards), top_value / len(shards))
        return jnp.repeat(jnp.exp(draws), extent[dim] // shards_of).reshape((-1,) + (1,) * (len(extent) - dim - 1))

    loudness = one(*shards[0])
    for cut in shards[1:]:
        loudness = loudness * one(*cut)
    return loudness


def centred(rng, extent, width, most, cuts=(), held_as=jnp.bfloat16):
    entries = width * jax.random.normal(rng, extent, jnp.float32)
    if cuts:
        entries = entries * levels(rng, extent, cuts, -0.22, 0.18)
    return jnp.clip(entries, -most, most).astype(held_as)


def setup_inputs(seed: int = 0) -> dict:
    key_list = jax.random.split(jax.random.key(seed), 13)
    return {
        "hidden_in": draw_hidden_in(jax.random.fold_in(key_list[12], 71), 0),
        "positions": draw_positions(jax.random.fold_in(key_list[12], 71), 0),
        "norm1_gain": jnp.clip(1.0 + 0.1 * jax.random.normal(key_list[2], (D,), jnp.float32), 0.5, 1.5),
        "q_weight": draw_q_weight(jax.random.fold_in(key_list[12], 71), 0),
        "k_weight": draw_k_weight(jax.random.fold_in(key_list[12], 71), 0),
        "v_weight": centred(key_list[5], (D * KW,), D ** -0.5, 0.1875, ((0, 32),)),
        "o_weight": centred(key_list[6], (QW * D,), (max(QW * 4 // MAXLEN, 1)) ** -0.5, 2.0, ((0, 32),)),
        "norm2_gain": jnp.clip(1.0 + 0.1 * jax.random.normal(key_list[7], (D,), jnp.float32), 0.5, 1.5),
        "gate_weight": centred(key_list[8], (D * FF,), D ** -0.5, 0.1875, ((0, 32),)),
        "up_weight": centred(key_list[9], (D * FF,), D ** -0.5, 0.1875, ((0, 32),)),
        "down_weight": centred(key_list[10], (FF * D,), (FF // 4) ** -0.5, 0.25, ((0, 32),)),
        "cotangent": centred(key_list[11], (TOKENS, D), 1.0, 6.0, ((0, 32),)),
    }


EPS = 1e-05
NEG_FILL = -1e+30

def rotary_tables(positions):
    half_width = HEAD_DIM // 2
    frequency = jnp.exp(jnp.arange(half_width, dtype=jnp.float32) * (-2.0 * math.log(10000.0) / HEAD_DIM))
    angles = positions.astype(jnp.float32)[:, None] * frequency[None, :]
    return (jnp.cos(angles), jnp.sin(angles))

def rotate(matrix, cosine, sine_table):
    row_count = matrix.shape[0]
    half_width = HEAD_DIM // 2
    shaped = matrix.reshape(row_count, -1, HEAD_DIM)
    first_half = shaped[:, :, :half_width]
    second_half = shaped[:, :, half_width:]
    cosine_rows = cosine[:, None, :]
    sine_rows = sine_table[:, None, :]
    turned = jnp.concatenate([first_half * cosine_rows - second_half * sine_rows, second_half * cosine_rows + first_half * sine_rows], axis=2)
    return turned.reshape(row_count, -1)

def norm_scale(matrix):
    return lax.rsqrt(lax.optimization_barrier(jnp.mean(matrix * matrix, axis=1, keepdims=True)) + EPS)

def norm_backward(matrix, scale_rows, gain, grad_normed):
    unit_rows = matrix * scale_rows
    weighted = grad_normed * gain[None, :]
    grad_gain = lax.optimization_barrier(jnp.sum(grad_normed * unit_rows, axis=0))
    grad_rows = scale_rows * (weighted - unit_rows * lax.optimization_barrier(jnp.mean(weighted * unit_rows, axis=1, keepdims=True)))
    return (grad_rows, grad_gain)

def score_block(query_block, key_block, position_block, prefix):
    row_count = query_block.shape[0]
    key_count = key_block.shape[0]
    grouped = query_block.astype(jnp.float32).reshape(row_count, KV_HEADS, GROUP, HEAD_DIM)
    key_heads = key_block.astype(jnp.float32).reshape(key_count, KV_HEADS, HEAD_DIM)
    scores = jnp.einsum('qkgd,skd->kgqs', grouped, key_heads) * HEAD_DIM ** (-0.5)
    key_offset = jnp.arange(key_count, dtype=jnp.int32) - prefix
    row_index = jnp.arange(row_count, dtype=jnp.int32)
    allowed = (key_offset[None, :] <= row_index[:, None]) & (key_offset[None, :] >= row_index[:, None] - position_block[:, None])
    return jnp.where(allowed[None, None], scores, NEG_FILL)

def attend(query_block, key_block, value_block, position_block, prefix):
    row_count = query_block.shape[0]
    key_count = key_block.shape[0]
    scores = score_block(query_block, key_block, position_block, prefix)
    row_max = lax.optimization_barrier(jnp.max(scores, axis=3, keepdims=True))
    log_total = row_max + jnp.log(lax.optimization_barrier(jnp.sum(jnp.exp(scores - row_max), axis=3, keepdims=True)))
    prob_low = jnp.exp(scores - log_total).astype(jnp.bfloat16)
    value_heads = value_block.astype(jnp.float32).reshape(key_count, KV_HEADS, HEAD_DIM)
    mixed_out = jnp.einsum('kgqs,skd->qkgd', prob_low.astype(jnp.float32), value_heads)
    return (mixed_out.reshape(row_count, -1).astype(jnp.bfloat16), log_total)

def attend_back(query_block, key_block, value_block, position_block, prefix, log_total, attended_block, grad_block):
    row_count = query_block.shape[0]
    key_count = key_block.shape[0]
    scores = score_block(query_block, key_block, position_block, prefix)
    prob_full = jnp.exp(scores - log_total)
    prob_low = prob_full.astype(jnp.bfloat16).astype(jnp.float32)
    grouped = query_block.astype(jnp.float32).reshape(row_count, KV_HEADS, GROUP, HEAD_DIM)
    grad_grouped = grad_block.astype(jnp.float32).reshape(row_count, KV_HEADS, GROUP, HEAD_DIM)
    out_grouped = attended_block.astype(jnp.float32).reshape(row_count, KV_HEADS, GROUP, HEAD_DIM)
    key_heads = key_block.astype(jnp.float32).reshape(key_count, KV_HEADS, HEAD_DIM)
    value_heads = value_block.astype(jnp.float32).reshape(key_count, KV_HEADS, HEAD_DIM)
    grad_prob = jnp.einsum('qkgd,skd->kgqs', grad_grouped, value_heads)
    delta_sum = jnp.einsum('qkgd,qkgd->kgq', grad_grouped, out_grouped)[..., None]
    grad_score = (prob_full * (grad_prob - delta_sum) * HEAD_DIM ** (-0.5)).astype(jnp.bfloat16).astype(jnp.float32)
    grad_query = jnp.einsum('kgqs,skd->qkgd', grad_score, key_heads).reshape(row_count, -1)
    grad_key = jnp.einsum('kgqs,qkgd->skd', grad_score, grouped).reshape(key_count, -1)
    grad_value = jnp.einsum('kgqs,qkgd->skd', prob_low, grad_grouped).reshape(key_count, -1)
    return (grad_query, grad_key, grad_value)

def reference(hidden_in, positions, norm1_gain, q_weight, k_weight, v_weight, o_weight, norm2_gain, gate_weight, up_weight, down_weight, cotangent):
    weight_query = q_weight.reshape(D, QW)
    weight_key = k_weight.reshape(D, KW)
    weight_value = v_weight.reshape(D, KW)
    weight_out = o_weight.reshape(QW, D)
    weight_gate = gate_weight.reshape(D, FF)
    weight_up = up_weight.reshape(D, FF)
    weight_down = down_weight.reshape(FF, D)
    input_rows = hidden_in.astype(jnp.float32)
    scale_one = norm_scale(input_rows)
    normed_one = (input_rows * scale_one * norm1_gain[None, :]).astype(jnp.bfloat16)
    cosine, sine_table = rotary_tables(positions)
    query_low = rotate(jnp.dot(normed_one, weight_query, preferred_element_type=jnp.float32), cosine, sine_table).astype(jnp.bfloat16)
    key_low = rotate(jnp.dot(normed_one, weight_key, preferred_element_type=jnp.float32), cosine, sine_table).astype(jnp.bfloat16)
    value_low = jnp.dot(normed_one, weight_value, preferred_element_type=jnp.float32).astype(jnp.bfloat16)
    block_rows = 4 * TOK_DEV
    prefix = SPAN * TOK_DEV
    blocks = TOKENS // block_rows
    key_pad = jnp.concatenate([jnp.zeros((prefix, KW), jnp.bfloat16), key_low], axis=0)
    value_pad = jnp.concatenate([jnp.zeros((prefix, KW), jnp.bfloat16), value_low], axis=0)
    starts = jnp.arange(blocks, dtype=jnp.int32) * block_rows

    def forward_block(start_row):
        query_block = lax.dynamic_slice_in_dim(query_low, start_row, block_rows, 0)
        position_block = lax.dynamic_slice_in_dim(positions, start_row, block_rows, 0)
        key_block = lax.dynamic_slice_in_dim(key_pad, start_row, block_rows + prefix, 0)
        value_block = lax.dynamic_slice_in_dim(value_pad, start_row, block_rows + prefix, 0)
        return attend(query_block, key_block, value_block, position_block, prefix)
    attended_parts, log_parts = lax.map(forward_block, starts)
    attended_low = attended_parts.reshape(TOKENS, QW)
    mid_rows = input_rows + jnp.dot(attended_low, weight_out, preferred_element_type=jnp.float32)
    scale_two = norm_scale(mid_rows)
    normed_two = (mid_rows * scale_two * norm2_gain[None, :]).astype(jnp.bfloat16)
    gate_pre = jnp.dot(normed_two, weight_gate, preferred_element_type=jnp.float32)
    up_pre = jnp.dot(normed_two, weight_up, preferred_element_type=jnp.float32)
    sigmoid_gate = jax.nn.sigmoid(gate_pre)
    silu_gate = gate_pre * sigmoid_gate
    hidden_low = (silu_gate * up_pre).astype(jnp.bfloat16)
    block_out = (mid_rows + jnp.dot(hidden_low, weight_down, preferred_element_type=jnp.float32)).astype(jnp.bfloat16)
    grad_down = jnp.dot(hidden_low.T, cotangent, preferred_element_type=jnp.float32)
    grad_hidden = jnp.dot(cotangent, weight_down.T, preferred_element_type=jnp.float32)
    grad_gate_low = (grad_hidden * up_pre * sigmoid_gate * (1.0 + gate_pre * (1.0 - sigmoid_gate))).astype(jnp.bfloat16)
    grad_up_low = (grad_hidden * silu_gate).astype(jnp.bfloat16)
    grad_gate = jnp.dot(normed_two.T, grad_gate_low, preferred_element_type=jnp.float32)
    grad_up = jnp.dot(normed_two.T, grad_up_low, preferred_element_type=jnp.float32)
    grad_normed_two = jnp.dot(grad_gate_low, weight_gate.T, preferred_element_type=jnp.float32) + jnp.dot(grad_up_low, weight_up.T, preferred_element_type=jnp.float32)
    grad_mid_norm, grad_gain_two = norm_backward(mid_rows, scale_two, norm2_gain, grad_normed_two)
    grad_mid = cotangent.astype(jnp.float32) + grad_mid_norm
    grad_mid_low = grad_mid.astype(jnp.bfloat16)
    grad_out = jnp.dot(attended_low.T, grad_mid_low, preferred_element_type=jnp.float32)
    grad_attended_low = jnp.dot(grad_mid_low, weight_out.T, preferred_element_type=jnp.float32).astype(jnp.bfloat16)
    grad_parts = grad_attended_low.reshape(blocks, block_rows, QW)

    def backward_block(carried, inputs):
        grad_key_pad, grad_value_pad = carried
        start_row, log_block, attended_block, grad_block = inputs
        query_block = lax.dynamic_slice_in_dim(query_low, start_row, block_rows, 0)
        position_block = lax.dynamic_slice_in_dim(positions, start_row, block_rows, 0)
        key_block = lax.dynamic_slice_in_dim(key_pad, start_row, block_rows + prefix, 0)
        value_block = lax.dynamic_slice_in_dim(value_pad, start_row, block_rows + prefix, 0)
        grad_query, grad_key, grad_value = attend_back(query_block, key_block, value_block, position_block, prefix, log_block, attended_block, grad_block)
        old_key = lax.dynamic_slice_in_dim(grad_key_pad, start_row, block_rows + prefix, 0)
        old_value = lax.dynamic_slice_in_dim(grad_value_pad, start_row, block_rows + prefix, 0)
        grad_key_pad = lax.dynamic_update_slice_in_dim(grad_key_pad, old_key + grad_key, start_row, 0)
        grad_value_pad = lax.dynamic_update_slice_in_dim(grad_value_pad, old_value + grad_value, start_row, 0)
        return ((grad_key_pad, grad_value_pad), grad_query)
    empty_pad = jnp.zeros((TOKENS + prefix, KW), jnp.float32)
    (grad_key_pad, grad_value_pad), grad_query_parts = lax.scan(backward_block, (empty_pad, empty_pad), (starts, log_parts, attended_parts, grad_parts))
    grad_query_all = grad_query_parts.reshape(TOKENS, QW)
    grad_query_in = rotate(grad_query_all, cosine, -sine_table).astype(jnp.bfloat16)
    grad_key_in = rotate(grad_key_pad[prefix:], cosine, -sine_table).astype(jnp.bfloat16)
    grad_value_in = grad_value_pad[prefix:].astype(jnp.bfloat16)
    grad_query_weight = jnp.dot(normed_one.T, grad_query_in, preferred_element_type=jnp.float32)
    grad_key_weight = jnp.dot(normed_one.T, grad_key_in, preferred_element_type=jnp.float32)
    grad_value_weight = jnp.dot(normed_one.T, grad_value_in, preferred_element_type=jnp.float32)
    grad_normed_one = jnp.dot(grad_query_in, weight_query.T, preferred_element_type=jnp.float32)
    grad_normed_one = grad_normed_one + jnp.dot(grad_key_in, weight_key.T, preferred_element_type=jnp.float32)
    grad_normed_one = grad_normed_one + jnp.dot(grad_value_in, weight_value.T, preferred_element_type=jnp.float32)
    grad_in_norm, grad_gain_one = norm_backward(input_rows, scale_one, norm1_gain, grad_normed_one)
    grad_in = (grad_mid + grad_in_norm).astype(jnp.bfloat16)
    return (block_out, grad_in, grad_gain_one, grad_query_weight.reshape(-1), grad_key_weight.reshape(-1), grad_value_weight.reshape(-1), grad_out.reshape(-1), grad_gain_two, grad_gate.reshape(-1), grad_up.reshape(-1), grad_down.reshape(-1))
```

```python
import math

import jax
import jax.numpy as jnp
from jax import lax
from jax.sharding import PartitionSpec as P

KV_HEADS = 5
HEAD_DIM = 64
MAXLEN = 512


EPS = 1e-05
NEG_FILL = -1e30
AXIS = "fsdp"
TEAM_BITS = (1, 2)
TEAM = 1 << len(TEAM_BITS)
LOW_BITS = 3
ROW_TILE = 16
LINK = jnp.bfloat16


def swap(block, mask):
    size = lax.axis_size(AXIS)
    return lax.ppermute(block, AXIS, [(i, i ^ mask) for i in range(size)])


def passed_along(block, distance):
    devices = range(lax.axis_size(AXIS))
    route = [(i - distance, i) for i in devices if i - distance in devices]
    return lax.ppermute(block, AXIS, route)


def pick(stack, index, axis=0):
    return lax.dynamic_index_in_dim(stack, index, axis, keepdims=False)


def team_masks():
    masks = []
    for member in range(TEAM):
        masks.append(sum(((member >> j) & 1) << bit for j, bit in enumerate(TEAM_BITS)))
    return masks


def rotary_tables(positions):
    half_width = HEAD_DIM // 2
    frequency = jnp.exp(
        jnp.arange(half_width, dtype=jnp.float32) * (-2.0 * math.log(10000.0) / HEAD_DIM)
    )
    angles = positions.astype(jnp.float32)[:, None] * frequency[None, :]
    return (jnp.cos(angles), jnp.sin(angles))


def rotate(matrix, cosine, sine_table):
    row_count = matrix.shape[0]
    half_width = HEAD_DIM // 2
    shaped = matrix.reshape(row_count, -1, HEAD_DIM)
    first_half = shaped[:, :, :half_width]
    second_half = shaped[:, :, half_width:]
    cosine_rows = cosine[:, None, :]
    sine_rows = sine_table[:, None, :]
    turned = jnp.concatenate(
        [
            first_half * cosine_rows - second_half * sine_rows,
            second_half * cosine_rows + first_half * sine_rows,
        ],
        axis=2,
    )
    return turned.reshape(row_count, -1)


def norm_scale(matrix):
    return lax.rsqrt(jnp.mean(matrix * matrix, axis=1, keepdims=True) + EPS)


def norm_backward(matrix, scale_rows, gain, grad_normed):
    unit_rows = matrix * scale_rows
    weighted = grad_normed * gain[None, :]
    grad_gain = jnp.sum(grad_normed * unit_rows, axis=0)
    grad_rows = scale_rows * (
        weighted - unit_rows * jnp.mean(weighted * unit_rows, axis=1, keepdims=True)
    )
    return (grad_rows, grad_gain)


def outer_sum(left_side, right_side):
    return lax.dot_general(
        left_side, right_side, (((0,), (0,)), ((), ())), preferred_element_type=jnp.float32
    )


def back_product(left_side, weight):
    return lax.dot_general(
        left_side, weight, (((1,), (1,)), ((), ())), preferred_element_type=jnp.float32
    )


def forward_product(left_side, weight):
    return jnp.dot(left_side, weight, preferred_element_type=jnp.float32)


def score_block(query_block, key_block, position_block, prefix):
    row_count = query_block.shape[0]
    key_count = key_block.shape[0]
    grouped = query_block.reshape(row_count, KV_HEADS, -1, HEAD_DIM)
    key_heads = key_block.reshape(key_count, KV_HEADS, HEAD_DIM)
    scores = jnp.einsum(
        "qkgd,skd->kgqs", grouped, key_heads, preferred_element_type=jnp.float32
    ) * HEAD_DIM ** (-0.5)
    key_offset = jnp.arange(key_count, dtype=jnp.int32) - prefix
    row_index = jnp.arange(row_count, dtype=jnp.int32)
    allowed = (key_offset[None, :] <= row_index[:, None]) & (
        key_offset[None, :] >= row_index[:, None] - position_block[:, None]
    )
    return jnp.where(allowed[None, None], scores, NEG_FILL)


def attend(query_block, key_block, value_block, position_block, prefix):
    row_count = query_block.shape[0]
    key_count = key_block.shape[0]
    scores = score_block(query_block, key_block, position_block, prefix)
    row_max = jnp.max(scores, axis=3, keepdims=True)
    log_total = row_max + jnp.log(jnp.sum(jnp.exp(scores - row_max), axis=3, keepdims=True))
    prob_low = jnp.exp(scores - log_total).astype(jnp.bfloat16)
    value_heads = value_block.reshape(key_count, KV_HEADS, HEAD_DIM)
    mixed_out = jnp.einsum(
        "kgqs,skd->qkgd", prob_low, value_heads, preferred_element_type=jnp.float32
    )
    return (mixed_out.reshape(row_count, -1).astype(jnp.bfloat16), log_total)


def attend_back(
    query_block,
    key_block,
    value_block,
    position_block,
    prefix,
    log_total,
    attended_block,
    grad_block,
):
    row_count = query_block.shape[0]
    key_count = key_block.shape[0]
    scores = score_block(query_block, key_block, position_block, prefix)
    prob_full = jnp.exp(scores - log_total)
    prob_low = prob_full.astype(jnp.bfloat16)
    grouped = query_block.reshape(row_count, KV_HEADS, -1, HEAD_DIM)
    grad_grouped = grad_block.reshape(row_count, KV_HEADS, -1, HEAD_DIM)
    out_grouped = attended_block.reshape(row_count, KV_HEADS, -1, HEAD_DIM)
    key_heads = key_block.reshape(key_count, KV_HEADS, HEAD_DIM)
    value_heads = value_block.reshape(key_count, KV_HEADS, HEAD_DIM)
    grad_prob = jnp.einsum(
        "qkgd,skd->kgqs", grad_grouped, value_heads, preferred_element_type=jnp.float32
    )
    delta_sum = jnp.einsum(
        "qkgd,qkgd->kgq", grad_grouped, out_grouped, preferred_element_type=jnp.float32
    )[..., None]
    grad_score = (prob_full * (grad_prob - delta_sum) * HEAD_DIM ** (-0.5)).astype(jnp.bfloat16)
    grad_query = jnp.einsum(
        "kgqs,skd->qkgd", grad_score, key_heads, preferred_element_type=jnp.float32
    ).reshape(row_count, -1)
    grad_key = jnp.einsum(
        "kgqs,qkgd->skd", grad_score, grouped, preferred_element_type=jnp.float32
    ).reshape(key_count, -1)
    grad_value = jnp.einsum(
        "kgqs,qkgd->skd", prob_low, grad_grouped, preferred_element_type=jnp.float32
    ).reshape(key_count, -1)
    return (grad_query, grad_key, grad_value)


class RowPlan:
    def __init__(self, row_total):
        size = lax.axis_size(AXIS)
        self.unit = size // math.gcd(size, row_total)
        self.rows = self.unit * row_total // size
        self.pitch = -(-self.rows // ROW_TILE) * ROW_TILE
        self.row_total = row_total
        unit_bits = self.unit.bit_length() - 1
        self.low = list(range(unit_bits))
        free = [b for b in range(unit_bits, size.bit_length() - 1)]
        self.outer = [b for b in free if b >= LOW_BITS]
        self.team = [b for b in free if b in TEAM_BITS]
        self.last = [b for b in free if b < LOW_BITS and b not in TEAM_BITS]
        team_set = [0]
        for bit in self.team:
            team_set += [m | (1 << bit) for m in team_set]
        self.team_set = team_set
        offsets = [0]
        for bit in self.outer:
            offsets += [m ^ (1 << bit) for m in offsets]
        offsets = [m ^ t for t in team_set for m in offsets]
        for bit in self.last:
            offsets += [m ^ (1 << bit) for m in offsets]
        self.offsets = [m // self.unit for m in offsets]

    def selector(self, place):
        slots = jnp.arange(len(self.offsets) * self.pitch, dtype=jnp.int32)
        block = slots // self.pitch
        within = slots % self.pitch
        start = jnp.repeat(jnp.array(self.offsets, jnp.int32), self.pitch)
        row = ((place // self.unit) ^ start) * self.rows + within
        row = jnp.where(within < self.rows, row, -1)
        del block
        return (jnp.arange(self.row_total, dtype=jnp.int32)[:, None] == row[None, :]).astype(
            jnp.bfloat16
        )

    def local(self, flats, place):
        parts = []
        for flat in flats:
            for bit in self.low:
                other = swap(flat, 1 << bit)
                high = (place >> bit) & 1
                flat = jnp.concatenate(
                    [jnp.where(high == 1, other, flat), jnp.where(high == 1, flat, other)]
                )
            parts.append(flat.reshape(self.rows, -1))
        block = jnp.concatenate(parts, axis=1) if len(parts) > 1 else parts[0]
        return jnp.pad(block, ((0, self.pitch - self.rows), (0, 0)))

    def gather(self, flats, place):
        stack = self.local(flats, place)
        for bit in self.outer:
            stack = jnp.concatenate([stack, swap(stack, 1 << bit)])
        stack = jnp.concatenate([stack] + [swap(stack, m) for m in self.team_set[1:]])
        for bit in self.last:
            stack = jnp.concatenate([stack, swap(stack, 1 << bit)])
        return stack

    def scatter(self, stack, widths, place):
        for bit in reversed(self.last):
            half = stack.shape[0] // 2
            stack = stack[:half] + swap(stack[half:].astype(LINK), 1 << bit).astype(jnp.float32)
        members = stack.reshape(len(self.team_set), -1, stack.shape[1])
        total = members[0]
        for position, mask in enumerate(self.team_set):
            if mask:
                total = total + swap(members[position].astype(LINK), mask).astype(jnp.float32)
        stack = total
        for bit in reversed(self.outer):
            half = stack.shape[0] // 2
            stack = stack[:half] + swap(stack[half:].astype(LINK), 1 << bit).astype(jnp.float32)
        stack = stack[: self.rows]
        flats = []
        start = 0
        for width in widths:
            flat = stack[:, start : start + width].reshape(-1)
            start += width
            for bit in reversed(self.low):
                high = (place >> bit) & 1
                halves = flat.reshape(2, -1)
                flat = pick(halves, high) + swap(
                    pick(halves, 1 - high).astype(LINK), 1 << bit
                ).astype(jnp.float32)
            flats.append(flat)
        return flats


def team_gather(block):
    return jnp.concatenate([block] + [swap(block, mask) for mask in team_masks()[1:]])


def team_scatter(stack, tok_rows):
    total = stack[:tok_rows]
    for member, mask in enumerate(team_masks()):
        if mask:
            part = stack[member * tok_rows : (member + 1) * tok_rows]
            total = total + swap(part.astype(LINK), mask).astype(jnp.float32)
    return total


def outer_gather(stack):
    size = lax.axis_size(AXIS)
    stack = stack[None]
    for bit in range(LOW_BITS, size.bit_length() - 1):
        stack = jnp.concatenate([stack, swap(stack, 1 << bit)])
    return jnp.stack([stack, swap(stack, 1)])


def outer_scatter(stack, place):
    size = lax.axis_size(AXIS)
    core = place & 1
    total = pick(stack, core, 1) + swap(pick(stack, 1 - core, 1).astype(LINK), 1).astype(
        jnp.float32
    )
    for bit in reversed(range(LOW_BITS, size.bit_length() - 1)):
        high = (place >> bit) & 1
        halves = total.reshape((2, -1) + total.shape[1:])
        total = pick(halves, high) + swap(pick(halves, 1 - high).astype(LINK), 1 << bit).astype(
            jnp.float32
        )
    return total[0]


def local(
    hidden_in,
    positions,
    norm1_gain,
    q_weight,
    k_weight,
    v_weight,
    o_weight,
    norm2_gain,
    gate_weight,
    up_weight,
    down_weight,
    cotangent,
):
    tok_rows = hidden_in.shape[0]
    model_width = hidden_in.shape[1]
    device_count = lax.axis_size(AXIS)
    place = lax.axis_index(AXIS)
    member = (place >> TEAM_BITS[0]) & (TEAM - 1)
    outer_index = place >> LOW_BITS
    outer_count = device_count >> LOW_BITS
    window_span = (MAXLEN + tok_rows - 2) // tok_rows
    prefix = window_span * tok_rows
    q_width = q_weight.shape[0] * device_count // model_width
    k_width = k_weight.shape[0] * device_count // model_width
    ff_width = gate_weight.shape[0] * device_count // model_width
    team_width = ff_width // TEAM
    column_run = 2 * ff_width // device_count
    masks = team_masks()

    in_plan = RowPlan(model_width)
    out_plan = RowPlan(q_width)
    weight_in = in_plan.gather((q_weight, k_weight, v_weight), place)
    select_in = in_plan.selector(place)
    weight_out = out_plan.gather((o_weight,), place)
    select_out = out_plan.selector(place)

    shard_size = gate_weight.shape[0]
    piece_size = shard_size // TEAM
    piece_shape = (
        (piece_size // team_width, team_width) if piece_size % team_width == 0 else (piece_size,)
    )

    def column_runs(flat):
        return flat.reshape(-1, TEAM, column_run)

    runs = jnp.stack([column_runs(gate_weight), column_runs(up_weight)])
    arrived = jnp.stack(
        [
            swap(pick(runs, member ^ r, 2), masks[r]) if r else pick(runs, member, 2)
            for r in range(TEAM)
        ]
    )
    ordered = jnp.stack([pick(arrived, member ^ t) for t in range(TEAM)], axis=1)
    pair_rel = outer_gather(ordered.reshape((2, TEAM) + piece_shape))
    down_rel = outer_gather(down_weight.reshape(-1, model_width))
    core = place & 1

    def in_order(rel, core_axis):
        blocks = []
        for j in range(outer_count):
            pieces = [pick(pick(rel, core ^ c), outer_index ^ j) for c in range(2)]
            blocks.append(jnp.stack(pieces, axis=core_axis))
        return jnp.stack(blocks)

    pair = in_order(pair_rel, 2)
    weight_gate = pair[:, 0].reshape(model_width, team_width)
    weight_up = pair[:, 1].reshape(model_width, team_width)
    weight_down = in_order(down_rel, 0).reshape(team_width, model_width)
    cotangent_all = team_gather(cotangent)

    input_rows = hidden_in.astype(jnp.float32)
    scale_one = norm_scale(input_rows)
    normed_one = (input_rows * scale_one * norm1_gain[None, :]).astype(jnp.bfloat16)
    placed_one = forward_product(normed_one, select_in).astype(jnp.bfloat16)
    cosine, sine_table = rotary_tables(positions)
    projected = forward_product(placed_one, weight_in)
    rotated = rotate(projected[:, : q_width + k_width], cosine, sine_table).astype(jnp.bfloat16)
    query_low = rotated[:, :q_width]
    key_value = jnp.concatenate(
        [rotated[:, q_width:], projected[:, q_width + k_width :].astype(jnp.bfloat16)], axis=1
    )
    pieces = [passed_along(key_value, distance) for distance in range(window_span, 0, -1)]
    window = jnp.concatenate(pieces + [key_value], axis=0)
    key_window = window[:, :k_width]
    value_window = window[:, k_width:]
    attended_low, log_total = attend(query_low, key_window, value_window, positions, prefix)
    placed_attended = forward_product(attended_low, select_out).astype(jnp.bfloat16)
    mid_rows = input_rows + forward_product(placed_attended, weight_out)
    scale_two = norm_scale(mid_rows)
    normed_two = (mid_rows * scale_two * norm2_gain[None, :]).astype(jnp.bfloat16)

    normed_all = team_gather(normed_two)
    gate_pre = forward_product(normed_all, weight_gate)
    up_pre = forward_product(normed_all, weight_up)
    sigmoid_gate = jax.nn.sigmoid(gate_pre)
    silu_gate = gate_pre * sigmoid_gate
    hidden_low = (silu_gate * up_pre).astype(jnp.bfloat16)
    grad_hidden = back_product(cotangent_all, weight_down)
    grad_gate_low = (
        grad_hidden * up_pre * sigmoid_gate * (1.0 + gate_pre * (1.0 - sigmoid_gate))
    ).astype(jnp.bfloat16)
    grad_up_low = (grad_hidden * silu_gate).astype(jnp.bfloat16)
    grad_normed_two = team_scatter(
        back_product(grad_gate_low, weight_gate) + back_product(grad_up_low, weight_up), tok_rows
    )
    block_out = (
        mid_rows + team_scatter(forward_product(hidden_low, weight_down), tok_rows)
    ).astype(jnp.bfloat16)

    grad_down = outer_scatter(
        outer_sum(hidden_low, cotangent_all).reshape(outer_count, 2, -1, model_width), place
    ).reshape(-1)
    pair_shape = (outer_count, TEAM, 2) + piece_shape
    grad_pair = outer_scatter(
        jnp.stack(
            [
                jnp.moveaxis(outer_sum(normed_all, grad_low).reshape(pair_shape), 2, 1)
                for grad_low in (grad_gate_low, grad_up_low)
            ],
            axis=2,
        ),
        place,
    )
    returned = jnp.stack(
        [
            swap(pick(grad_pair, member ^ r, 1).astype(LINK), masks[r]).astype(jnp.float32)
            if r
            else pick(grad_pair, member, 1)
            for r in range(TEAM)
        ]
    ).reshape(TEAM, 2, -1, column_run)
    ordered_back = jnp.stack([pick(returned, member ^ t) for t in range(TEAM)], axis=2)
    grad_gate = ordered_back[0].reshape(-1)
    grad_up = ordered_back[1].reshape(-1)

    grad_mid_norm, grad_gain_two = norm_backward(mid_rows, scale_two, norm2_gain, grad_normed_two)
    grad_mid = cotangent.astype(jnp.float32) + grad_mid_norm
    grad_mid_low = grad_mid.astype(jnp.bfloat16)
    (grad_out,) = out_plan.scatter(outer_sum(placed_attended, grad_mid_low), (model_width,), place)
    grad_attended_low = back_product(
        back_product(grad_mid_low, weight_out).astype(jnp.bfloat16), select_out
    ).astype(jnp.bfloat16)
    grad_query, grad_key_window, grad_value_window = attend_back(
        query_low,
        key_window,
        value_window,
        positions,
        prefix,
        log_total,
        attended_low,
        grad_attended_low,
    )
    grad_window = jnp.concatenate([grad_key_window, grad_value_window], axis=1)
    own_pair = grad_window[prefix:]
    for distance in range(1, window_span + 1):
        start_row = prefix - distance * tok_rows
        part = grad_window[start_row : start_row + tok_rows].astype(LINK)
        own_pair = own_pair + passed_along(part, -distance).astype(jnp.float32)
    turned_back = rotate(
        jnp.concatenate([grad_query, own_pair[:, :k_width]], axis=1), cosine, -sine_table
    )
    grad_projected = jnp.concatenate([turned_back, own_pair[:, k_width:]], axis=1).astype(
        jnp.bfloat16
    )
    grad_query_weight, grad_key_weight, grad_value_weight = in_plan.scatter(
        outer_sum(placed_one, grad_projected), (q_width, k_width, k_width), place
    )
    grad_normed_one = lax.dot_general(
        back_product(grad_projected, weight_in),
        select_in.astype(jnp.float32),
        (((1,), (1,)), ((), ())),
        precision=lax.Precision.HIGHEST,
        preferred_element_type=jnp.float32,
    )
    grad_in_norm, grad_gain_one = norm_backward(input_rows, scale_one, norm1_gain, grad_normed_one)
    grad_in = (grad_mid + grad_in_norm).astype(jnp.bfloat16)
    gains = jnp.stack([grad_gain_one, grad_gain_two])
    for bit in range(device_count.bit_length() - 1):
        gains = gains + swap(gains, 1 << bit)
    return (
        block_out,
        grad_in,
        gains[0],
        grad_query_weight,
        grad_key_weight,
        grad_value_weight,
        grad_out,
        gains[1],
        grad_gate,
        grad_up,
        grad_down,
    )


def solution(mesh):
    placed = (
        P("fsdp", None),
        P("fsdp"),
        P(),
        P("fsdp"),
        P("fsdp"),
        P("fsdp"),
        P("fsdp"),
        P(),
        P("fsdp"),
        P("fsdp"),
        P("fsdp"),
        P("fsdp", None),
    )
    return jax.shard_map(
        local,
        mesh=mesh,
        in_specs=placed,
        out_specs=(
            P("fsdp", None),
            P("fsdp", None),
            P(),
            P("fsdp"),
            P("fsdp"),
            P("fsdp"),
            P("fsdp"),
            P(),
            P("fsdp"),
            P("fsdp"),
            P("fsdp"),
        ),
        check_vma=False,
    )
```

```python
import math

import jax
import jax.numpy as jnp
from jax import lax
from jax.experimental import pallas as pl
from jax.experimental.pallas import tpu as pltpu
from jax.sharding import PartitionSpec as P

KV_HEADS = 5
HEAD_DIM = 64
MAXLEN = 512


EPS = 1e-05
NEG_FILL = -1e30
AXIS = "fsdp"
TEAM_BITS = (1, 2)
TEAM = 1 << len(TEAM_BITS)
LOW_BITS = 3
ROW_TILE = 16
LINK = jnp.bfloat16


def swap(block, mask):
    size = lax.axis_size(AXIS)
    return lax.ppermute(block, AXIS, [(i, i ^ mask) for i in range(size)])


def passed_along(block, distance):
    devices = range(lax.axis_size(AXIS))
    route = [(i - distance, i) for i in devices if i - distance in devices]
    return lax.ppermute(block, AXIS, route)


def pick(stack, index, axis=0):
    return lax.dynamic_index_in_dim(stack, index, axis, keepdims=False)


def team_masks():
    masks = []
    for member in range(TEAM):
        masks.append(sum(((member >> j) & 1) << bit for j, bit in enumerate(TEAM_BITS)))
    return masks


def rotary_tables(positions):
    half_width = HEAD_DIM // 2
    frequency = jnp.exp(
        jnp.arange(half_width, dtype=jnp.float32) * (-2.0 * math.log(10000.0) / HEAD_DIM)
    )
    angles = positions.astype(jnp.float32)[:, None] * frequency[None, :]
    return (jnp.cos(angles), jnp.sin(angles))


def rotate(matrix, cosine, sine_table):
    row_count = matrix.shape[0]
    half_width = HEAD_DIM // 2
    shaped = matrix.reshape(row_count, -1, HEAD_DIM)
    first_half = shaped[:, :, :half_width]
    second_half = shaped[:, :, half_width:]
    cosine_rows = cosine[:, None, :]
    sine_rows = sine_table[:, None, :]
    turned = jnp.concatenate(
        [
            first_half * cosine_rows - second_half * sine_rows,
            second_half * cosine_rows + first_half * sine_rows,
        ],
        axis=2,
    )
    return turned.reshape(row_count, -1)


def norm_scale(matrix):
    return lax.rsqrt(jnp.mean(matrix * matrix, axis=1, keepdims=True) + EPS)


def norm_backward(matrix, scale_rows, gain, grad_normed):
    unit_rows = matrix * scale_rows
    weighted = grad_normed * gain[None, :]
    grad_gain = jnp.sum(grad_normed * unit_rows, axis=0)
    grad_rows = scale_rows * (
        weighted - unit_rows * jnp.mean(weighted * unit_rows, axis=1, keepdims=True)
    )
    return (grad_rows, grad_gain)


def outer_sum(left_side, right_side):
    return lax.dot_general(
        left_side, right_side, (((0,), (0,)), ((), ())), preferred_element_type=jnp.float32
    )


def back_product(left_side, weight):
    return lax.dot_general(
        left_side, weight, (((1,), (1,)), ((), ())), preferred_element_type=jnp.float32
    )


def forward_product(left_side, weight):
    return jnp.dot(left_side, weight, preferred_element_type=jnp.float32)


def score_block(query_block, key_block, position_block, prefix):
    row_count = query_block.shape[0]
    key_count = key_block.shape[0]
    grouped = query_block.reshape(row_count, KV_HEADS, -1, HEAD_DIM)
    key_heads = key_block.reshape(key_count, KV_HEADS, HEAD_DIM)
    scores = jnp.einsum(
        "qkgd,skd->kgqs", grouped, key_heads, preferred_element_type=jnp.float32
    ) * HEAD_DIM ** (-0.5)
    key_offset = jnp.arange(key_count, dtype=jnp.int32) - prefix
    row_index = jnp.arange(row_count, dtype=jnp.int32)
    allowed = (key_offset[None, :] <= row_index[:, None]) & (
        key_offset[None, :] >= row_index[:, None] - position_block[:, None]
    )
    return jnp.where(allowed[None, None], scores, NEG_FILL)


def attend(query_block, key_block, value_block, position_block, prefix):
    row_count = query_block.shape[0]
    key_count = key_block.shape[0]
    scores = score_block(query_block, key_block, position_block, prefix)
    row_max = jnp.max(scores, axis=3, keepdims=True)
    log_total = row_max + jnp.log(jnp.sum(jnp.exp(scores - row_max), axis=3, keepdims=True))
    prob_low = jnp.exp(scores - log_total).astype(jnp.bfloat16)
    value_heads = value_block.reshape(key_count, KV_HEADS, HEAD_DIM)
    mixed_out = jnp.einsum(
        "kgqs,skd->qkgd", prob_low, value_heads, preferred_element_type=jnp.float32
    )
    return (mixed_out.reshape(row_count, -1).astype(jnp.bfloat16), log_total)


def attend_back(
    query_block,
    key_block,
    value_block,
    position_block,
    prefix,
    log_total,
    attended_block,
    grad_block,
):
    row_count = query_block.shape[0]
    key_count = key_block.shape[0]
    scores = score_block(query_block, key_block, position_block, prefix)
    prob_full = jnp.exp(scores - log_total)
    prob_low = prob_full.astype(jnp.bfloat16)
    grouped = query_block.reshape(row_count, KV_HEADS, -1, HEAD_DIM)
    grad_grouped = grad_block.reshape(row_count, KV_HEADS, -1, HEAD_DIM)
    out_grouped = attended_block.reshape(row_count, KV_HEADS, -1, HEAD_DIM)
    key_heads = key_block.reshape(key_count, KV_HEADS, HEAD_DIM)
    value_heads = value_block.reshape(key_count, KV_HEADS, HEAD_DIM)
    grad_prob = jnp.einsum(
        "qkgd,skd->kgqs", grad_grouped, value_heads, preferred_element_type=jnp.float32
    )
    delta_sum = jnp.einsum(
        "qkgd,qkgd->kgq", grad_grouped, out_grouped, preferred_element_type=jnp.float32
    )[..., None]
    grad_score = (prob_full * (grad_prob - delta_sum) * HEAD_DIM ** (-0.5)).astype(jnp.bfloat16)
    grad_query = jnp.einsum(
        "kgqs,skd->qkgd", grad_score, key_heads, preferred_element_type=jnp.float32
    ).reshape(row_count, -1)
    grad_key = jnp.einsum(
        "kgqs,qkgd->skd", grad_score, grouped, preferred_element_type=jnp.float32
    ).reshape(key_count, -1)
    grad_value = jnp.einsum(
        "kgqs,qkgd->skd", prob_low, grad_grouped, preferred_element_type=jnp.float32
    ).reshape(key_count, -1)
    return (grad_query, grad_key, grad_value)


def product(left_side, right_side, left_dim, right_dim):
    return lax.dot_general(
        left_side,
        right_side,
        (((left_dim,), (right_dim,)), ((), ())),
        preferred_element_type=jnp.float32,
    )


def kernel_call(body, outs, operands):
    return pl.pallas_call(
        body,
        out_shape=[jax.ShapeDtypeStruct(shape, dtype) for shape, dtype in outs],
        compiler_params=pltpu.CompilerParams(vmem_limit_bytes=60 * 1024 * 1024),
    )(*operands)


def tie(*values):
    return lax.optimization_barrier(values)


def bit_groups(bits):
    return [bits[i : i + 2] for i in range(0, len(bits), 2)]


def group_masks(bits):
    masks = [0]
    for bit in bits:
        masks += [m | (1 << bit) for m in masks]
    return masks


def spread(block, masks):
    return [block] + [swap(block, mask) for mask in masks[1:]]


def reduce_split(own, received, count):
    rows = own.shape[0] // count
    width = own.shape[1]

    def body(*refs):
        total = refs[0][...]
        for ref in refs[1 : 1 + len(received)]:
            total = total + ref[...].astype(jnp.float32)
        for i, out in enumerate(refs[1 + len(received) :]):
            out[...] = total[i * rows : (i + 1) * rows].astype(out.dtype)

    outs = [((rows, width), jnp.float32 if i == 0 else LINK) for i in range(count)]
    return kernel_call(body, outs, [own] + list(received))


class RowPlan:
    def __init__(self, row_total):
        size = lax.axis_size(AXIS)
        self.unit = size // math.gcd(size, row_total)
        self.rows = self.unit * row_total // size
        self.pitch = -(-self.rows // ROW_TILE) * ROW_TILE
        self.row_total = row_total
        unit_bits = self.unit.bit_length() - 1
        self.low = list(range(unit_bits))
        free = list(range(unit_bits, size.bit_length() - 1))
        self.outer = bit_groups([b for b in free if b >= LOW_BITS])
        self.team = group_masks([b for b in free if b in TEAM_BITS])
        self.last = group_masks([b for b in free if b < LOW_BITS and b not in TEAM_BITS])
        self.outer_set = group_masks([b for group in self.outer for b in group])

    def selector(self, place, distances):
        start = jnp.repeat(
            jnp.array([m // self.unit for m in distances], jnp.int32), self.pitch
        )
        within = jnp.tile(jnp.arange(self.pitch, dtype=jnp.int32), len(distances))
        row = ((place // self.unit) ^ start) * self.rows + within
        row = jnp.where(within < self.rows, row, -1)
        return (jnp.arange(self.row_total, dtype=jnp.int32)[:, None] == row[None, :]).astype(
            jnp.bfloat16
        )

    def whole_rows(self, flat, place):
        for bit in self.low:
            other = swap(flat, 1 << bit)
            high = (place >> bit) & 1
            flat = jnp.concatenate(
                [jnp.where(high == 1, other, flat), jnp.where(high == 1, flat, other)]
            )
        return flat.reshape(self.rows, -1)

    def own_share(self, block, place):
        flat = block.reshape(-1)
        for bit in reversed(self.low):
            high = (place >> bit) & 1
            halves = flat.reshape(2, -1)
            flat = pick(halves, high) + swap(
                pick(halves, 1 - high).astype(LINK), 1 << bit
            ).astype(jnp.float32)
        return flat

    def padded(self, block):
        return jnp.pad(block, ((0, self.pitch - self.rows), (0, 0)))

    def outer_pieces(self, block):
        pieces = [block]
        for group in self.outer:
            block = jnp.concatenate(pieces) if len(pieces) > 1 else pieces[0]
            pieces = spread(block, group_masks(group))
        return pieces

    def outer_sum(self, own, blocks):
        for step, group in enumerate(reversed(self.outer)):
            masks = group_masks(group)
            arrived = [swap(b, m) for b, m in zip(blocks, masks[1:])]
            following = self.outer[len(self.outer) - 2 - step] if step + 1 < len(self.outer) else []
            own, *blocks = reduce_split(own, arrived, 1 << len(following))
        return own


def pair_project(tokens, select, pieces):
    rows = tokens[0].shape[0]
    count = len(tokens)
    width = pieces[0].shape[1]
    depth = pieces[0].shape[0]

    def body(*refs):
        select_ref = refs[count]
        weights = refs[count + 1 : count + 1 + len(pieces)]
        outs = refs[count + 1 + len(pieces) :]
        for i in range(count):
            placed = product(refs[i][...], select_ref[...], 1, 0).astype(jnp.bfloat16)
            outs[count][i * rows : (i + 1) * rows, :] = placed
            total = product(placed[:, :depth], weights[0][...], 1, 0)
            for j in range(1, len(pieces)):
                total += product(placed[:, j * depth : (j + 1) * depth], weights[j][...], 1, 0)
            outs[i][...] = total

    outs = [((rows, width), jnp.float32)] * count
    outs.append(((count * rows, select.shape[1]), jnp.bfloat16))
    results = kernel_call(body, outs, list(tokens) + [select] + list(pieces))
    return results[:count], results[count]


def pair_back(grads, placed, select, pieces):
    count = len(grads)
    rows = grads[0].shape[0]
    width = pieces[0].shape[1]
    depth = pieces[0].shape[0]
    features = select.shape[0]

    def body(*refs):
        placed_ref, select_ref = refs[count : count + 2]
        weights = refs[count + 2 : count + 2 + len(pieces)]
        outs = refs[count + 2 + len(pieces) :]
        for j in range(len(pieces)):
            total = None
            for i in range(count):
                part = product(
                    placed_ref[i * rows : (i + 1) * rows, j * depth : (j + 1) * depth],
                    refs[i][...],
                    0,
                    0,
                )
                total = part if total is None else total + part
            outs[j][...] = total.astype(outs[j].dtype)
        for i in range(count):
            total = None
            for j in range(len(pieces)):
                back = product(refs[i][...], weights[j][...], 1, 1)
                high = back.astype(jnp.bfloat16)
                rest = (back - high.astype(jnp.float32)).astype(jnp.bfloat16)
                chosen = select_ref[:, j * depth : (j + 1) * depth]
                part = product(high, chosen, 1, 1) + product(rest, chosen, 1, 1)
                total = part if total is None else total + part
            outs[len(pieces) + i][...] = total

    outs = [((depth, width), jnp.float32 if j == 0 else LINK) for j in range(len(pieces))]
    outs += [((rows, features), jnp.float32)] * count
    results = kernel_call(body, outs, list(grads) + [placed, select] + list(pieces))
    return results[: len(pieces)], results[len(pieces) :]


def feed_forward(normed_blocks, cotangent_blocks, select, pair_pieces, down_pieces, order):
    count = len(normed_blocks)
    rows, features = normed_blocks[0].shape
    total_rows = count * rows
    depth, both = pair_pieces[0].shape
    width = both // 2
    down_rows = down_pieces[0].shape[0]
    pair_count = len(pair_pieces)
    down_count = len(down_pieces)

    def body(*refs):
        at = 0
        normed = refs[at : at + count]
        at += count
        grads = refs[at : at + count]
        at += count
        select_ref = refs[at]
        at += 1
        weights = refs[at : at + pair_count]
        at += pair_count
        downs = refs[at : at + down_count]
        at += down_count
        order_ref = refs[at]
        placed_out, hidden_out, low_out, *back_outs = refs[at + 1 :]
        down = product(
            order_ref[...], jnp.concatenate([d[...] for d in downs], axis=0), 1, 0
        ).astype(jnp.bfloat16)
        for i in range(count):
            span = slice(i * rows, (i + 1) * rows)
            placed = product(normed[i][...], select_ref[...], 1, 0).astype(jnp.bfloat16)
            placed_out[span, :] = placed
            total = product(placed[:, :depth], weights[0][...], 1, 0)
            for j in range(1, pair_count):
                total += product(placed[:, j * depth : (j + 1) * depth], weights[j][...], 1, 0)
            gate_pre = total[:, :width]
            up_pre = total[:, width:]
            sigmoid_gate = 1.0 / (1.0 + jnp.exp(-gate_pre))
            silu_gate = gate_pre * sigmoid_gate
            hidden = (silu_gate * up_pre).astype(jnp.bfloat16)
            hidden_out[span, :] = product(hidden, order_ref[...], 1, 0).astype(jnp.bfloat16)
            grad_hidden = product(grads[i][...], down, 1, 1)
            low_out[span, :width] = (
                grad_hidden * up_pre * sigmoid_gate * (1.0 + gate_pre * (1.0 - sigmoid_gate))
            ).astype(jnp.bfloat16)
            low_out[span, width:] = (grad_hidden * silu_gate).astype(jnp.bfloat16)
        for i in range(count):
            low = low_out[i * rows : (i + 1) * rows, :]
            total = None
            for j in range(pair_count):
                back = product(low, weights[j][...], 1, 1).astype(jnp.bfloat16)
                part = product(back, select_ref[:, j * depth : (j + 1) * depth], 1, 1)
                total = part if total is None else total + part
            back_outs[i][...] = total.astype(LINK)

    outs = [
        ((total_rows, select.shape[1]), jnp.bfloat16),
        ((total_rows, width), jnp.bfloat16),
        ((total_rows, both), jnp.bfloat16),
    ] + [((rows, features), LINK)] * count
    operands = list(normed_blocks) + list(cotangent_blocks) + [select]
    operands += list(pair_pieces) + list(down_pieces) + [order]
    results = kernel_call(body, outs, operands)
    return results[0], results[1], results[2], results[3:]


def split_products(left_side, right_blocks, first_rows):
    count = len(right_blocks)
    all_rows = left_side.shape[1]
    width = right_blocks[0].shape[1]
    step = right_blocks[0].shape[0]

    def body(*refs):
        left_ref = refs[0]
        outs = refs[1 + count :]
        for j, out in enumerate(outs):
            span = slice(0, first_rows) if j == 0 else slice(first_rows, all_rows)
            total = None
            for i in range(count):
                part = product(
                    left_ref[i * step : (i + 1) * step, span], refs[1 + i][...], 0, 0
                )
                total = part if total is None else total + part
            out[...] = total.astype(out.dtype)

    outs = [((first_rows, width), jnp.float32)]
    if first_rows < all_rows:
        outs.append(((all_rows - first_rows, width), LINK))
    return kernel_call(body, outs, [left_side] + list(right_blocks))


def block_products(left_side, down_pieces, count):
    rows = left_side.shape[0] // count
    width = down_pieces[0].shape[1]

    def body(*refs):
        down = jnp.concatenate([d[...] for d in refs[1 : 1 + len(down_pieces)]], axis=0)
        for i, out in enumerate(refs[1 + len(down_pieces) :]):
            part = product(refs[0][i * rows : (i + 1) * rows, :], down, 1, 0)
            out[...] = part.astype(out.dtype)

    outs = [((rows, width), jnp.float32 if i == 0 else LINK) for i in range(count)]
    return kernel_call(body, outs, [left_side] + list(down_pieces))


def local(
    hidden_in,
    positions,
    norm1_gain,
    q_weight,
    k_weight,
    v_weight,
    o_weight,
    norm2_gain,
    gate_weight,
    up_weight,
    down_weight,
    cotangent,
):
    tok_rows = hidden_in.shape[0]
    model_width = hidden_in.shape[1]
    device_count = lax.axis_size(AXIS)
    place = lax.axis_index(AXIS)
    member = (place >> TEAM_BITS[0]) & (TEAM - 1)
    outer_index = place >> LOW_BITS
    core = place & 1
    outer_bits = device_count.bit_length() - 1 - LOW_BITS
    top_shift = outer_bits - len(TEAM_BITS)
    window_span = (MAXLEN + tok_rows - 2) // tok_rows
    prefix = window_span * tok_rows
    q_width = q_weight.shape[0] * device_count // model_width
    k_width = k_weight.shape[0] * device_count // model_width
    ff_width = gate_weight.shape[0] * device_count // model_width
    team_width = ff_width // TEAM
    down_rows = ff_width // device_count
    masks = team_masks()

    in_plan = RowPlan(model_width)
    out_plan = RowPlan(q_width)
    paired = len(in_plan.last) > 1

    def both_cores(block):
        return [block, swap(block, 1)] if paired else [block]

    def pair_total(outs):
        return outs[0] + swap(outs[1], 1) if paired else outs[0]

    def distances(plan):
        return [t ^ o for t in plan.team for o in plan.outer_set]

    input_rows = hidden_in.astype(jnp.float32)
    scale_one = norm_scale(input_rows)
    normed_one = (input_rows * scale_one * norm1_gain[None, :]).astype(jnp.bfloat16)
    normed_pair = both_cores(normed_one)

    in_block = in_plan.padded(
        jnp.concatenate([in_plan.whole_rows(w, place) for w in (q_weight, k_weight, v_weight)], 1)
    )
    in_outer = jnp.concatenate(in_plan.outer_pieces(in_block))
    in_outer, o_flat, gate_flat, up_flat, down_flat = tie(
        in_outer, o_weight, gate_weight, up_weight, down_weight
    )
    weight_in = spread(in_outer, in_plan.team)
    select_in = in_plan.selector(place, distances(in_plan))
    out_outer = jnp.concatenate(
        out_plan.outer_pieces(out_plan.padded(out_plan.whole_rows(o_flat, place)))
    )
    select_out = out_plan.selector(place, distances(out_plan))

    def traded(i):
        outer, mem, c = i >> LOW_BITS, (i >> TEAM_BITS[0]) & (TEAM - 1), i & 1
        inner = outer & ((1 << top_shift) - 1)
        return (((mem << top_shift) | inner) << LOW_BITS) | ((outer >> top_shift) << TEAM_BITS[0]) | c

    trade_route = [(i, traded(i)) for i in range(device_count)]
    chunk_start = []
    for c in range(2):
        for o in in_plan.outer_set:
            o_from = outer_index ^ (o >> LOW_BITS)
            inner = o_from & ((1 << top_shift) - 1)
            chunk = (inner << LOW_BITS) | ((o_from >> top_shift) << TEAM_BITS[0]) | (core ^ c)
            chunk_start.append(chunk * down_rows)
    column = jnp.repeat(jnp.stack(chunk_start), down_rows) + jnp.tile(
        jnp.arange(down_rows, dtype=jnp.int32), len(chunk_start)
    )
    select_unit = (
        jnp.arange(team_width, dtype=jnp.int32)[:, None] == column[None, :]
    ).astype(jnp.bfloat16)

    def slabs(flat):
        whole = in_plan.whole_rows(flat, place)
        parts = jnp.concatenate(
            [whole[:, t * team_width : (t + 1) * team_width] for t in range(TEAM)]
        )
        return parts.reshape(TEAM, -1, team_width)

    gap = in_plan.pitch - in_plan.rows
    pair_slabs = jnp.pad(
        jnp.concatenate([slabs(gate_flat), slabs(up_flat)], axis=2), ((0, 0), (0, gap), (0, 0))
    )
    member_shift = [m >> TEAM_BITS[0] for m in in_plan.team]
    arrived = [
        swap(pick(pair_slabs, member ^ s), m) if m else pick(pair_slabs, member)
        for s, m in zip(member_shift, in_plan.team)
    ]
    pair_outer = in_plan.outer_pieces(jnp.concatenate(arrived))
    weight_pair = pair_outer + [swap(p, m) for m in in_plan.last[1:] for p in pair_outer]
    ff_distances = [c ^ o ^ t for c in in_plan.last for o in in_plan.outer_set for t in in_plan.team]
    select_ff = in_plan.selector(place, ff_distances)
    down_block = lax.ppermute(down_flat.reshape(down_rows, model_width), AXIS, trade_route)
    down_half = jnp.concatenate(in_plan.outer_pieces(down_block))
    weight_down = [down_half, swap(down_half, 1)]

    cosine, sine_table = rotary_tables(positions)
    projected_pair, placed_one = pair_project(normed_pair, select_in, weight_in)
    projected = pair_total(projected_pair)
    out_outer, cotangent_late, projected = tie(out_outer, cotangent, projected)
    weight_out = spread(out_outer, out_plan.team)
    rotated = rotate(projected[:, : q_width + k_width], cosine, sine_table).astype(jnp.bfloat16)
    query_low = rotated[:, :q_width]
    key_value = jnp.concatenate(
        [rotated[:, q_width:], projected[:, q_width + k_width :].astype(jnp.bfloat16)], axis=1
    )
    pieces = [passed_along(key_value, distance) for distance in range(window_span, 0, -1)]
    window = jnp.concatenate(pieces + [key_value], axis=0)
    cotangent_blocks = spread(cotangent_late, masks)
    key_window = window[:, :k_width]
    value_window = window[:, k_width:]
    attended_low, log_total = attend(query_low, key_window, value_window, positions, prefix)
    mixed_pair, placed_attended = pair_project(both_cores(attended_low), select_out, weight_out)
    mid_rows = input_rows + pair_total(mixed_pair)
    scale_two = norm_scale(mid_rows)
    normed_two = (mid_rows * scale_two * norm2_gain[None, :]).astype(jnp.bfloat16)

    normed_blocks = spread(normed_two, masks)
    placed_two, hidden_low, grad_low, back_blocks = feed_forward(
        normed_blocks, cotangent_blocks, select_ff, weight_pair, weight_down, select_unit
    )
    grad_normed_two = back_blocks[0].astype(jnp.float32)
    for block, mask in zip(back_blocks[1:], masks[1:]):
        grad_normed_two = grad_normed_two + swap(block, mask).astype(jnp.float32)

    low_blocks = [grad_low]
    pair_rows = placed_two.shape[1] // len(in_plan.last)
    pair_grads = split_products(placed_two, low_blocks, pair_rows)
    pair_arrived = [swap(g, m) for g, m in zip(pair_grads[1:], in_plan.last[1:])]
    down_grads = split_products(
        hidden_low, [jnp.concatenate(cotangent_blocks)], team_width // 2
    )
    down_arrived = [swap(down_grads[1], 1)]
    outer_group = 1 << len(in_plan.outer[-1])
    pair_own, *pair_blocks = reduce_split(pair_grads[0], pair_arrived, outer_group)
    down_own, *down_blocks = reduce_split(down_grads[0], down_arrived, outer_group)
    grad_mid_norm, grad_gain_two = norm_backward(mid_rows, scale_two, norm2_gain, grad_normed_two)
    grad_mid = cotangent.astype(jnp.float32) + grad_mid_norm
    grad_mid, pair_blocks, down_blocks, hidden_late = tie(
        grad_mid, pair_blocks, down_blocks, hidden_low
    )
    out_blocks = block_products(hidden_late, weight_down, TEAM)
    out_total = out_blocks[0]
    for block, mask in zip(out_blocks[1:], masks[1:]):
        out_total = out_total + swap(block, mask).astype(jnp.float32)
    block_out = (mid_rows + out_total).astype(jnp.bfloat16)

    pair_sum = in_plan.outer_sum(pair_own, pair_blocks)
    down_sum = in_plan.outer_sum(down_own, down_blocks)
    grad_down = lax.ppermute(down_sum.astype(LINK), AXIS, trade_route).astype(jnp.float32).reshape(-1)
    pair_blocks_t = pair_sum.reshape(len(in_plan.team), in_plan.pitch, 2 * team_width)
    returned = [
        swap(pair_blocks_t[i].astype(LINK), m) if m else pair_blocks_t[i].astype(LINK)
        for i, m in enumerate(in_plan.team)
    ]
    back_stack = jnp.stack(returned)[:, : in_plan.rows]
    natural = (back_stack[:, :, :team_width], back_stack[:, :, team_width:])

    def owned(grad_slabs):
        columns = []
        for t in range(TEAM):
            column_part = jnp.zeros_like(grad_slabs[0])
            for i, s in enumerate(member_shift):
                column_part = jnp.where((member ^ s) == t, grad_slabs[i], column_part)
            columns.append(column_part)
        return in_plan.own_share(
            jnp.concatenate(columns, axis=1).astype(jnp.float32), place
        )

    grad_gate = owned(natural[0])
    grad_up = owned(natural[1])

    grad_mid_low = grad_mid.astype(jnp.bfloat16)
    out_grads, attended_pair = pair_back(
        both_cores(grad_mid_low), placed_attended, select_out, weight_out
    )
    grad_attended_low = pair_total(attended_pair).astype(jnp.bfloat16)

    def weight_share(plan, grads):
        arrived_blocks = [swap(g, m) for g, m in zip(grads[1:], plan.team[1:])]
        own, *blocks = reduce_split(grads[0], arrived_blocks, 1 << len(plan.outer[-1]))
        return plan.outer_sum(own, blocks)[: plan.rows]

    grad_out = out_plan.own_share(weight_share(out_plan, out_grads), place)
    grad_query, grad_key_window, grad_value_window = attend_back(
        query_low,
        key_window,
        value_window,
        positions,
        prefix,
        log_total,
        attended_low,
        grad_attended_low,
    )
    grad_window = jnp.concatenate([grad_key_window, grad_value_window], axis=1)
    own_pair = grad_window[prefix:]
    for distance in range(1, window_span + 1):
        start_row = prefix - distance * tok_rows
        part = grad_window[start_row : start_row + tok_rows].astype(LINK)
        own_pair = own_pair + passed_along(part, -distance).astype(jnp.float32)
    turned_back = rotate(
        jnp.concatenate([grad_query, own_pair[:, :k_width]], axis=1), cosine, -sine_table
    )
    grad_projected = jnp.concatenate([turned_back, own_pair[:, k_width:]], axis=1).astype(
        jnp.bfloat16
    )
    in_grads, normed_grads = pair_back(
        both_cores(grad_projected), placed_one, select_in, weight_in
    )
    in_share = weight_share(in_plan, in_grads)
    grad_query_weight = in_plan.own_share(in_share[:, :q_width], place)
    grad_key_weight = in_plan.own_share(in_share[:, q_width : q_width + k_width], place)
    grad_value_weight = in_plan.own_share(in_share[:, q_width + k_width :], place)
    grad_normed_one = pair_total(normed_grads)
    grad_in_norm, grad_gain_one = norm_backward(input_rows, scale_one, norm1_gain, grad_normed_one)
    grad_in = (grad_mid + grad_in_norm).astype(jnp.bfloat16)
    gains = jnp.stack([grad_gain_one, grad_gain_two])
    for bit in range(device_count.bit_length() - 1):
        gains = gains + swap(gains, 1 << bit)
    return (
        block_out,
        grad_in,
        gains[0],
        grad_query_weight,
        grad_key_weight,
        grad_value_weight,
        grad_out,
        gains[1],
        grad_gate,
        grad_up,
        grad_down,
    )


def solution(mesh):
    placed = (
        P("fsdp", None),
        P("fsdp"),
        P(),
        P("fsdp"),
        P("fsdp"),
        P("fsdp"),
        P("fsdp"),
        P(),
        P("fsdp"),
        P("fsdp"),
        P("fsdp"),
        P("fsdp", None),
    )
    return jax.shard_map(
        local,
        mesh=mesh,
        in_specs=placed,
        out_specs=(
            P("fsdp", None),
            P("fsdp", None),
            P(),
            P("fsdp"),
            P("fsdp"),
            P("fsdp"),
            P("fsdp"),
            P(),
            P("fsdp"),
            P("fsdp"),
            P("fsdp"),
        ),
        check_vma=False,
    )
```

```python
import math

import jax
import jax.numpy as jnp
from jax import lax
from jax.experimental import pallas as pl
from jax.experimental.pallas import tpu as pltpu
from jax.sharding import PartitionSpec as P


KV_HEADS = 5
HEAD_DIM = 64
MAXLEN = 512


EPS = 1e-05
NEG_FILL = -1e30
AXIS = "fsdp"
TEAM_BITS = (1, 2)
TEAM = 1 << len(TEAM_BITS)
LOW_BITS = 3
ROW_TILE = 16
LINK = jnp.bfloat16
LANES = 128


def swap(block, mask):
    size = lax.axis_size(AXIS)
    return lax.ppermute(block, AXIS, [(i, i ^ mask) for i in range(size)])


def passed_along(block, distance):
    devices = range(lax.axis_size(AXIS))
    route = [(i - distance, i) for i in devices if i - distance in devices]
    return lax.ppermute(block, AXIS, route)


def pick(stack, index, axis=0):
    return lax.dynamic_index_in_dim(stack, index, axis, keepdims=False)


def team_masks():
    masks = []
    for member in range(TEAM):
        masks.append(sum(((member >> j) & 1) << bit for j, bit in enumerate(TEAM_BITS)))
    return masks


def rotary_tables(positions):
    half_width = HEAD_DIM // 2
    frequency = jnp.exp(
        jnp.arange(half_width, dtype=jnp.float32) * (-2.0 * math.log(10000.0) / HEAD_DIM)
    )
    angles = positions.astype(jnp.float32)[:, None] * frequency[None, :]
    repeats = LANES // half_width
    return (jnp.tile(jnp.cos(angles), (1, repeats)), jnp.tile(jnp.sin(angles), (1, repeats)))


def rotate(matrix, cosine, sine_table):
    half_width = HEAD_DIM // 2
    lane = lax.broadcasted_iota(jnp.int32, cosine.shape, 1)
    first_half = lane % HEAD_DIM < half_width
    signed = jnp.where(first_half, -sine_table, sine_table)
    turned = []
    for start in range(0, matrix.shape[1], LANES):
        part = matrix[:, start : start + LANES]
        other = jnp.where(
            first_half,
            pltpu.roll(part, LANES - half_width, 1),
            pltpu.roll(part, half_width, 1),
        )
        turned.append(part * cosine + other * signed)
    return jnp.concatenate(turned, axis=1)


def norm_scale(matrix):
    return lax.rsqrt(jnp.mean(matrix * matrix, axis=1, keepdims=True) + EPS)


def norm_backward(matrix, scale_rows, gain, grad_normed):
    unit_rows = matrix * scale_rows
    weighted = grad_normed * gain[None, :]
    grad_gain = jnp.sum(grad_normed * unit_rows, axis=0)
    grad_rows = scale_rows * (
        weighted - unit_rows * jnp.mean(weighted * unit_rows, axis=1, keepdims=True)
    )
    return (grad_rows, grad_gain)


def back_product(left_side, weight):
    return lax.dot_general(
        left_side, weight, (((1,), (1,)), ((), ())), preferred_element_type=jnp.float32
    )


def forward_product(left_side, weight):
    return jnp.dot(left_side, weight, preferred_element_type=jnp.float32)


def product(left_side, right_side, left_dim, right_dim):
    return lax.dot_general(
        left_side,
        right_side,
        (((left_dim,), (right_dim,)), ((), ())),
        preferred_element_type=jnp.float32,
    )


def kernel_call(body, outs, operands):
    return pl.pallas_call(
        body,
        out_shape=[jax.ShapeDtypeStruct(shape, dtype) for shape, dtype in outs],
        compiler_params=pltpu.CompilerParams(vmem_limit_bytes=60 * 1024 * 1024),
    )(*operands)


def tie(*values):
    return lax.optimization_barrier(values)


def bit_groups(bits):
    return [bits[i : i + 2] for i in range(0, len(bits), 2)]


def group_masks(bits):
    masks = [0]
    for bit in bits:
        masks += [m | (1 << bit) for m in masks]
    return masks


def spread(block, masks):
    return [block] + [swap(block, mask) for mask in masks[1:]]


def reduce_split(own, received, count):
    rows = own.shape[0] // count
    width = own.shape[1]

    def body(*refs):
        total = refs[0][...]
        for ref in refs[1 : 1 + len(received)]:
            total = total + ref[...].astype(jnp.float32)
        for i, out in enumerate(refs[1 + len(received) :]):
            out[...] = total[i * rows : (i + 1) * rows].astype(out.dtype)

    outs = [((rows, width), jnp.float32 if i == 0 else LINK) for i in range(count)]
    return kernel_call(body, outs, [own] + list(received))


class RowPlan:
    def __init__(self, row_total):
        size = lax.axis_size(AXIS)
        self.unit = size // math.gcd(size, row_total)
        self.rows = self.unit * row_total // size
        self.pitch = -(-self.rows // ROW_TILE) * ROW_TILE
        self.row_total = row_total
        unit_bits = self.unit.bit_length() - 1
        self.low = list(range(unit_bits))
        free = list(range(unit_bits, size.bit_length() - 1))
        self.outer = bit_groups([b for b in free if b >= LOW_BITS])
        self.team = group_masks([b for b in free if b in TEAM_BITS])
        self.last = group_masks([b for b in free if b < LOW_BITS and b not in TEAM_BITS])
        self.outer_set = group_masks([b for group in self.outer for b in group])

    def selector(self, base, distances):
        start = jnp.repeat(
            jnp.array([m // self.unit for m in distances], jnp.int32), self.pitch
        )
        within = jnp.tile(jnp.arange(self.pitch, dtype=jnp.int32), len(distances))
        row = ((base // self.unit) ^ start) * self.rows + within
        row = jnp.where(within < self.rows, row, -1)
        return (jnp.arange(self.row_total, dtype=jnp.int32)[:, None] == row[None, :]).astype(
            jnp.bfloat16
        )

    def whole_rows(self, flat, place):
        for bit in self.low:
            other = swap(flat, 1 << bit)
            high = (place >> bit) & 1
            flat = jnp.concatenate(
                [jnp.where(high == 1, other, flat), jnp.where(high == 1, flat, other)]
            )
        return flat.reshape(self.rows, -1)

    def own_share(self, block, place):
        flat = block.reshape(-1)
        for bit in reversed(self.low):
            high = (place >> bit) & 1
            halves = flat.reshape(2, -1)
            flat = pick(halves, high) + swap(
                pick(halves, 1 - high).astype(LINK), 1 << bit
            ).astype(jnp.float32)
        return flat

    def padded(self, block):
        return jnp.pad(block, ((0, self.pitch - self.rows), (0, 0)))

    def outer_pieces(self, block):
        pieces = [block]
        for group in self.outer:
            block = jnp.concatenate(pieces) if len(pieces) > 1 else pieces[0]
            pieces = spread(block, group_masks(group))
        return pieces

    def outer_send(self, blocks):
        return [swap(b, m) for b, m in zip(blocks, group_masks(self.outer[-1])[1:])]

    def outer_sum(self, own, arrived):
        for step, group in enumerate(reversed(self.outer)):
            following = self.outer[len(self.outer) - 2 - step] if step + 1 < len(self.outer) else []
            own, *blocks = reduce_split(own, arrived, 1 << len(following))
            arrived = [swap(b, m) for b, m in zip(blocks, group_masks(following)[1:])]
        return own


def pair_project(tokens, select, pieces):
    rows = tokens[0].shape[0]
    count = len(tokens)
    width = pieces[0].shape[1]
    depth = pieces[0].shape[0]

    def body(*refs):
        select_ref = refs[count]
        weights = refs[count + 1 : count + 1 + len(pieces)]
        outs = refs[count + 1 + len(pieces) :]
        tokens_all = jnp.concatenate([refs[i][...] for i in range(count)], axis=0)
        placed = product(tokens_all, select_ref[...], 1, 0).astype(jnp.bfloat16)
        outs[count][...] = placed
        total = product(placed[:, :depth], weights[0][...], 1, 0)
        for j in range(1, len(pieces)):
            total += product(placed[:, j * depth : (j + 1) * depth], weights[j][...], 1, 0)
        for i in range(count):
            outs[i][...] = total[i * rows : (i + 1) * rows]

    outs = [((rows, width), jnp.float32)] * count
    outs.append(((count * rows, select.shape[1]), jnp.bfloat16))
    results = kernel_call(body, outs, list(tokens) + [select] + list(pieces))
    return results[:count], results[count]


def pair_back(grads, placed, select, pieces):
    count = len(grads)
    rows = grads[0].shape[0]
    width = pieces[0].shape[1]
    depth = pieces[0].shape[0]
    features = select.shape[0]

    def body(*refs):
        placed_ref, select_ref = refs[count : count + 2]
        weights = refs[count + 2 : count + 2 + len(pieces)]
        outs = refs[count + 2 + len(pieces) :]
        grads_all = jnp.concatenate([refs[i][...] for i in range(count)], axis=0)
        total = None
        for j in range(len(pieces)):
            span = slice(j * depth, (j + 1) * depth)
            outs[j][...] = product(placed_ref[:, span], grads_all, 0, 0).astype(outs[j].dtype)
            back = product(grads_all, weights[j][...], 1, 1)
            high = back.astype(jnp.bfloat16)
            rest = (back - high.astype(jnp.float32)).astype(jnp.bfloat16)
            chosen = select_ref[:, span]
            part = product(high, chosen, 1, 1) + product(rest, chosen, 1, 1)
            total = part if total is None else total + part
        for i in range(count):
            outs[len(pieces) + i][...] = total[i * rows : (i + 1) * rows]

    outs = [((depth, width), jnp.float32 if j == 0 else LINK) for j in range(len(pieces))]
    outs += [((rows, features), jnp.float32)] * count
    results = kernel_call(body, outs, list(grads) + [placed, select] + list(pieces))
    return results[: len(pieces)], results[len(pieces) :]


def feed_forward(normed_blocks, cotangent_blocks, pair_pieces, down):
    count = len(normed_blocks)
    rows, features = normed_blocks[0].shape
    total_rows = count * rows
    depth, both = pair_pieces[0].shape
    width = both // 2
    pair_count = len(pair_pieces)

    def body(*refs):
        weights = refs[2 * count : 2 * count + pair_count]
        down_ref = refs[2 * count + pair_count]
        hidden_out, low_out, *back_outs = refs[2 * count + pair_count + 1 :]
        placed = jnp.concatenate([refs[i][...] for i in range(count)], axis=0)
        grads = jnp.concatenate([refs[count + i][...] for i in range(count)], axis=0)
        total = product(placed[:, :depth], weights[0][...], 1, 0)
        for j in range(1, pair_count):
            total += product(placed[:, j * depth : (j + 1) * depth], weights[j][...], 1, 0)
        gate_pre = total[:, :width]
        up_pre = total[:, width:]
        sigmoid_gate = 1.0 / (1.0 + jnp.exp(-gate_pre))
        silu_gate = gate_pre * sigmoid_gate
        hidden_out[...] = (silu_gate * up_pre).astype(jnp.bfloat16)
        grad_hidden = product(grads, down_ref[...], 1, 1)
        low_out[:, :width] = (
            grad_hidden * up_pre * sigmoid_gate * (1.0 + gate_pre * (1.0 - sigmoid_gate))
        ).astype(jnp.bfloat16)
        low_out[:, width:] = (grad_hidden * silu_gate).astype(jnp.bfloat16)
        low = low_out[...]
        for j in range(pair_count):
            back = product(low, weights[j][...], 1, 1)
            for i in range(count):
                part = back[i * rows : (i + 1) * rows]
                back_outs[i][:, j * depth : (j + 1) * depth] = part.astype(back_outs[i].dtype)

    outs = [((total_rows, width), jnp.bfloat16), ((total_rows, both), jnp.bfloat16)]
    outs += [((rows, features), jnp.float32 if i == 0 else LINK) for i in range(count)]
    operands = list(normed_blocks) + list(cotangent_blocks) + list(pair_pieces) + [down]
    results = kernel_call(body, outs, operands)
    return results[0], results[1], results[2:]


def split_products(left_blocks, right_side, first_rows):
    count = len(left_blocks)
    all_rows = left_blocks[0].shape[1]
    width = right_side.shape[1]

    def body(*refs):
        left = jnp.concatenate([refs[i][...] for i in range(count)], axis=0)
        right = refs[count][...]
        refs[count + 1][...] = product(left[:, :first_rows], right, 0, 0)
        if first_rows < all_rows:
            refs[count + 2][...] = product(left[:, first_rows:], right, 0, 0).astype(LINK)

    outs = [((first_rows, width), jnp.float32)]
    if first_rows < all_rows:
        outs.append(((all_rows - first_rows, width), LINK))
    return kernel_call(body, outs, list(left_blocks) + [right_side])


def turn(projected_parts, tables, q_width, k_width):
    rows = projected_parts[0].shape[0]
    count = len(projected_parts)

    def body(*refs):
        cosine_ref, sine_ref, query_out, pair_out = refs[count:]
        total = refs[0][...]
        for ref in refs[1:count]:
            total = total + ref[...]
        turned = rotate(total[:, : q_width + k_width], cosine_ref[...], sine_ref[...])
        query_out[...] = turned[:, :q_width].astype(jnp.bfloat16)
        pair_out[...] = jnp.concatenate(
            [turned[:, q_width:], total[:, q_width + k_width :]], axis=1
        ).astype(jnp.bfloat16)

    outs = [((rows, q_width), jnp.bfloat16), ((rows, 2 * k_width), jnp.bfloat16)]
    return kernel_call(body, outs, list(projected_parts) + list(tables))


def turn_back(grad_query, pair_parts, tables):
    rows, q_width = grad_query.shape
    k_width = pair_parts[0].shape[1] // 2

    def body(query_ref, cosine_ref, sine_ref, *refs):
        *parts, out = refs
        total = parts[0][...]
        for ref in parts[1:]:
            total = total + ref[...].astype(jnp.float32)
        heads = jnp.concatenate([query_ref[...], total[:, :k_width]], axis=1)
        turned = rotate(heads, cosine_ref[...], -sine_ref[...])
        out[...] = jnp.concatenate([turned, total[:, k_width:]], axis=1).astype(jnp.bfloat16)

    outs = [((rows, q_width + 2 * k_width), jnp.bfloat16)]
    return kernel_call(body, outs, [grad_query] + list(tables) + list(pair_parts))[0]


def allowed_pairs(position_ref, row_count, key_count, prefix):
    key_offset = lax.broadcasted_iota(jnp.int32, (row_count, key_count), 1) - prefix
    row_index = lax.broadcasted_iota(jnp.int32, (row_count, key_count), 0)
    return (key_offset <= row_index) & (key_offset >= row_index - position_ref[...])


def group_rows(ref, group, size):
    start = group * size * HEAD_DIM
    return jnp.concatenate(
        [ref[:, start + h * HEAD_DIM : start + (h + 1) * HEAD_DIM] for h in range(size)], axis=0
    )


def side_by_side(stacked, row_count):
    return [stacked[h * row_count : (h + 1) * row_count] for h in range(stacked.shape[0] // row_count)]


def attend(query_block, window_blocks, position_block, prefix):
    row_count, q_width = query_block.shape
    k_width = window_blocks[0].shape[1] // 2
    key_count = len(window_blocks) * row_count
    group_size = q_width // k_width

    def body(query_ref, position_ref, *refs):
        *window_refs, out_ref, log_ref = refs
        window = jnp.concatenate([ref[...] for ref in window_refs], axis=0)
        allowed = allowed_pairs(position_ref, row_count, key_count, prefix)
        fill = jnp.where(allowed, 0.0, NEG_FILL)
        fill = jnp.concatenate([fill] * group_size, axis=0)
        columns = []
        for g in range(KV_HEADS):
            span = slice(g * HEAD_DIM, (g + 1) * HEAD_DIM)
            scores = product(group_rows(query_ref, g, group_size), window[:, span], 1, 1)
            scores = jnp.where(fill < 0.0, NEG_FILL, scores * HEAD_DIM ** (-0.5))
            row_max = jnp.max(scores, axis=1, keepdims=True)
            total = jnp.sum(jnp.exp(scores - row_max), axis=1, keepdims=True)
            log_total = row_max + jnp.log(total)
            log_ref[g] = log_total
            prob_low = jnp.exp(scores - log_total).astype(jnp.bfloat16)
            values = window[:, k_width + g * HEAD_DIM : k_width + (g + 1) * HEAD_DIM]
            columns += side_by_side(product(prob_low, values, 1, 0), row_count)
        out_ref[...] = jnp.concatenate(columns, axis=1).astype(jnp.bfloat16)

    outs = [
        ((row_count, q_width), jnp.bfloat16),
        ((KV_HEADS, group_size * row_count, 1), jnp.float32),
    ]
    operands = [query_block, position_block[:, None]] + list(window_blocks)
    return kernel_call(body, outs, operands)


def attend_back(
    query_block, window_blocks, position_block, prefix, log_total, attended_block, grad_block
):
    row_count, q_width = query_block.shape
    k_width = window_blocks[0].shape[1] // 2
    count = len(window_blocks)
    key_count = count * row_count
    group_size = q_width // k_width

    def body(query_ref, position_ref, log_ref, attended_ref, grad_ref, *refs):
        window_refs = refs[:count]
        query_out, *window_outs = refs[count:]
        window = jnp.concatenate([ref[...] for ref in window_refs], axis=0)
        allowed = allowed_pairs(position_ref, row_count, key_count, prefix)
        fill = jnp.where(allowed, 0.0, NEG_FILL)
        fill = jnp.concatenate([fill] * group_size, axis=0)
        query_columns = []
        key_columns = []
        value_columns = []
        for g in range(KV_HEADS):
            span = slice(g * HEAD_DIM, (g + 1) * HEAD_DIM)
            keys = window[:, span]
            values = window[:, k_width + g * HEAD_DIM : k_width + (g + 1) * HEAD_DIM]
            queries = group_rows(query_ref, g, group_size)
            grads = group_rows(grad_ref, g, group_size)
            outputs = group_rows(attended_ref, g, group_size)
            scores = product(queries, keys, 1, 1)
            scores = jnp.where(fill < 0.0, NEG_FILL, scores * HEAD_DIM ** (-0.5))
            prob_full = jnp.exp(scores - log_ref[g])
            grad_prob = product(grads, values, 1, 1)
            delta_sum = jnp.sum(
                grads.astype(jnp.float32) * outputs.astype(jnp.float32), axis=1, keepdims=True
            )
            grad_score = (prob_full * (grad_prob - delta_sum) * HEAD_DIM ** (-0.5)).astype(
                jnp.bfloat16
            )
            query_columns += side_by_side(product(grad_score, keys, 1, 0), row_count)
            key_columns.append(product(grad_score, queries, 0, 0))
            value_columns.append(product(prob_full.astype(jnp.bfloat16), grads, 0, 0))
        query_out[...] = jnp.concatenate(query_columns, axis=1)
        total = jnp.concatenate(key_columns + value_columns, axis=1)
        for i, out in enumerate(window_outs):
            out[...] = total[i * row_count : (i + 1) * row_count].astype(out.dtype)

    outs = [((row_count, q_width), jnp.float32)]
    outs += [
        ((row_count, 2 * k_width), jnp.float32 if i == count - 1 else LINK) for i in range(count)
    ]
    operands = [query_block, position_block[:, None], log_total, attended_block, grad_block]
    results = kernel_call(body, outs, operands + list(window_blocks))
    return results[0], results[1:]


def starts_call(body, outs, starts, operands, scratch=()):
    return pl.pallas_call(
        body,
        out_shape=[jax.ShapeDtypeStruct(shape, dtype) for shape, dtype in outs],
        in_specs=[pl.BlockSpec(memory_space=pltpu.SMEM)]
        + [pl.BlockSpec(memory_space=pltpu.VMEM)] * len(operands),
        scratch_shapes=list(scratch),
        compiler_params=pltpu.CompilerParams(vmem_limit_bytes=60 * 1024 * 1024),
    )(starts, *operands)


def arrange_rows(pieces, starts, chunk, order):
    total = sum(piece.shape[0] for piece in pieces)
    width = pieces[0].shape[1]
    if chunk % ROW_TILE:
        stacked = jnp.concatenate(pieces)
        return forward_product(order, stacked).astype(jnp.bfloat16)
    per_piece = pieces[0].shape[0] // chunk

    def body(starts_ref, *refs):
        for j in range(total // chunk):
            at = pl.multiple_of(starts_ref[j], ROW_TILE)
            start = (j % per_piece) * chunk
            refs[-1][pl.ds(at, chunk), :] = refs[j // per_piece][start : start + chunk, :]

    return starts_call(body, [((total, width), jnp.bfloat16)], starts, list(pieces))[0]


def down_products(hidden, grads, starts, chunk, order):
    if chunk % ROW_TILE:
        placed = forward_product(hidden, order).astype(jnp.bfloat16)
        return split_products([placed], jnp.concatenate(grads), hidden.shape[1] // 2)
    half = hidden.shape[1] // 2
    width = grads[0].shape[1]
    count = len(grads)

    def body(starts_ref, *refs):
        hidden_ref = refs[0]
        own, other, total_ref = refs[1 + count :]
        right = jnp.concatenate([refs[1 + i][...] for i in range(count)], axis=0)
        total_ref[...] = product(hidden_ref[...], right, 0, 0)
        for j in range(2 * half // chunk):
            rows = total_ref[pl.ds(pl.multiple_of(starts_ref[j], ROW_TILE), chunk), :]
            target = own if j * chunk < half else other
            start = j * chunk % half
            target[start : start + chunk, :] = rows.astype(target.dtype)

    outs = [((half, width), jnp.float32), ((half, width), LINK)]
    scratch = [pltpu.VMEM((2 * half, width), jnp.float32)]
    return starts_call(body, outs, starts, [hidden] + list(grads), scratch)


def block_products(left_side, down, count):
    rows = left_side.shape[0] // count
    width = down.shape[1]

    def body(left_ref, down_ref, *outs):
        total = product(left_ref[...], down_ref[...], 1, 0)
        for i, out in enumerate(outs):
            out[...] = total[i * rows : (i + 1) * rows].astype(out.dtype)

    outs = [((rows, width), jnp.float32 if i == 0 else LINK) for i in range(count)]
    return kernel_call(body, outs, [left_side, down])


def local(
    hidden_in,
    positions,
    norm1_gain,
    q_weight,
    k_weight,
    v_weight,
    o_weight,
    norm2_gain,
    gate_weight,
    up_weight,
    down_weight,
    cotangent,
):
    tok_rows = hidden_in.shape[0]
    model_width = hidden_in.shape[1]
    device_count = lax.axis_size(AXIS)
    place = lax.axis_index(AXIS)
    member = (place >> TEAM_BITS[0]) & (TEAM - 1)
    outer_index = place >> LOW_BITS
    core = place & 1
    outer_bits = device_count.bit_length() - 1 - LOW_BITS
    top_shift = outer_bits - len(TEAM_BITS)
    window_span = (MAXLEN + tok_rows - 2) // tok_rows
    prefix = window_span * tok_rows
    q_width = q_weight.shape[0] * device_count // model_width
    k_width = k_weight.shape[0] * device_count // model_width
    ff_width = gate_weight.shape[0] * device_count // model_width
    team_width = ff_width // TEAM
    down_rows = ff_width // device_count
    masks = team_masks()

    in_plan = RowPlan(model_width)
    out_plan = RowPlan(q_width)
    paired = len(in_plan.last) > 1

    def both_cores(block):
        return [block, swap(block, 1)] if paired else [block]

    def pair_total(outs):
        return outs[0] + swap(outs[1], 1) if paired else outs[0]

    def distances(plan):
        return [t ^ o for t in plan.team for o in plan.outer_set]

    input_rows = hidden_in.astype(jnp.float32)
    scale_one = norm_scale(input_rows)
    normed_one = (input_rows * scale_one * norm1_gain[None, :]).astype(jnp.bfloat16)
    normed_pair = both_cores(normed_one)

    in_block = in_plan.padded(
        jnp.concatenate([in_plan.whole_rows(w, place) for w in (q_weight, k_weight, v_weight)], 1)
    )
    in_outer = jnp.concatenate(in_plan.outer_pieces(in_block))
    select_in = in_plan.selector(place, distances(in_plan))
    select_out = out_plan.selector(place, distances(out_plan))

    def traded(i):
        outer, mem, c = i >> LOW_BITS, (i >> TEAM_BITS[0]) & (TEAM - 1), i & 1
        inner = outer & ((1 << top_shift) - 1)
        return (((mem << top_shift) | inner) << LOW_BITS) | ((outer >> top_shift) << TEAM_BITS[0]) | c

    trade_route = [(i, traded(i)) for i in range(device_count)]
    chunk_start = []
    for c in range(2):
        for o in in_plan.outer_set:
            o_from = outer_index ^ (o >> LOW_BITS)
            inner = o_from & ((1 << top_shift) - 1)
            chunk = (inner << LOW_BITS) | ((o_from >> top_shift) << TEAM_BITS[0]) | (core ^ c)
            chunk_start.append(chunk * down_rows)
    column = jnp.repeat(jnp.stack(chunk_start), down_rows) + jnp.tile(
        jnp.arange(down_rows, dtype=jnp.int32), len(chunk_start)
    )
    unit_starts = jnp.stack(chunk_start).astype(jnp.int32)
    select_unit = (
        jnp.arange(team_width, dtype=jnp.int32)[:, None] == column[None, :]
    ).astype(jnp.bfloat16)

    def slabs(flat):
        whole = in_plan.whole_rows(flat, place)
        parts = jnp.concatenate(
            [whole[:, t * team_width : (t + 1) * team_width] for t in range(TEAM)]
        )
        return parts.reshape(TEAM, -1, team_width)

    gap = in_plan.pitch - in_plan.rows
    pair_slabs = jnp.pad(
        jnp.concatenate([slabs(gate_weight), slabs(up_weight)], axis=2), ((0, 0), (0, gap), (0, 0))
    )
    member_shift = [m >> TEAM_BITS[0] for m in in_plan.team]
    arrived = [
        swap(pick(pair_slabs, member ^ s), m) if m else pick(pair_slabs, member)
        for s, m in zip(member_shift, in_plan.team)
    ]
    team_index = sum(
        ((place >> (m.bit_length() - 1)) & 1) << i
        for i, m in enumerate(m for m in in_plan.team if m & (m - 1) == 0 and m)
    )
    arrived = jnp.stack(arrived)
    pair_block = jnp.concatenate(
        [pick(arrived, team_index ^ i) for i in range(len(in_plan.team))]
    )
    down_block = lax.ppermute(down_weight.reshape(down_rows, model_width), AXIS, trade_route)
    _, pair_block, down_block, o_flat = tie(in_outer, pair_block, down_block, o_weight)
    weight_in = spread(in_outer, in_plan.team)
    out_pieces = out_plan.outer_pieces(out_plan.padded(out_plan.whole_rows(o_flat, place)))
    pair_outer = in_plan.outer_pieces(pair_block)
    down_outer = in_plan.outer_pieces(down_block)
    out_outer = jnp.concatenate(out_pieces)
    weight_pair = pair_outer + [swap(p, m) for m in in_plan.last[1:] for p in pair_outer]
    ff_distances = [c ^ o ^ t for c in in_plan.last for o in in_plan.outer_set for t in in_plan.team]
    select_ff = in_plan.selector(place & ~in_plan.team[-1], ff_distances)
    weight_down = arrange_rows(
        down_outer + [swap(piece, 1) for piece in down_outer], unit_starts, down_rows, select_unit
    )

    tables = rotary_tables(positions)
    projected_pair, placed_one = pair_project(normed_pair, select_in, weight_in)
    projected_parts = list(projected_pair[:1]) + [swap(part, 1) for part in projected_pair[1:]]
    out_outer, cotangent_late, _ = tie(out_outer, cotangent, projected_parts)
    weight_out = spread(out_outer, out_plan.team)
    query_low, key_value = turn(projected_parts, tables, q_width, k_width)
    pieces = [passed_along(key_value, distance) for distance in range(window_span, 0, -1)]
    cotangent_blocks = spread(cotangent_late, masks)
    window_blocks = pieces + [key_value]
    attended_low, log_total = attend(query_low, window_blocks, positions, prefix)
    mixed_pair, placed_attended = pair_project(both_cores(attended_low), select_out, weight_out)
    mid_rows = input_rows + pair_total(mixed_pair)
    scale_two = norm_scale(mid_rows)
    normed_two = (mid_rows * scale_two * norm2_gain[None, :]).astype(jnp.bfloat16)

    placed_two = forward_product(normed_two, select_ff).astype(jnp.bfloat16)
    normed_blocks = spread(placed_two, masks)
    hidden_low, grad_low, back_blocks = feed_forward(
        normed_blocks, cotangent_blocks, weight_pair, weight_down
    )
    back_total = back_blocks[0]
    for block, mask in zip(back_blocks[1:], masks[1:]):
        back_total = back_total + swap(block, mask).astype(jnp.float32)
    back_high = lax.reduce_precision(back_total, 8, 7)
    grad_normed_two = back_product(back_high.astype(jnp.bfloat16), select_ff) + back_product(
        (back_total - back_high).astype(jnp.bfloat16), select_ff
    )

    pair_rows = placed_two.shape[1] // len(in_plan.last)
    pair_grads = split_products(normed_blocks, grad_low, pair_rows)
    pair_arrived = [swap(g, m) for g, m in zip(pair_grads[1:], in_plan.last[1:])]
    down_grads = down_products(
        hidden_low, cotangent_blocks, unit_starts, down_rows, select_unit
    )
    down_arrived = [swap(down_grads[1], 1)]
    outer_group = 1 << len(in_plan.outer[-1])
    pair_own, *pair_blocks = reduce_split(pair_grads[0], pair_arrived, outer_group)
    down_own, *down_blocks = reduce_split(down_grads[0], down_arrived, outer_group)
    pair_sent = in_plan.outer_send(pair_blocks)
    down_sent = in_plan.outer_send(down_blocks)
    grad_mid_norm, grad_gain_two = norm_backward(mid_rows, scale_two, norm2_gain, grad_normed_two)
    grad_mid = cotangent.astype(jnp.float32) + grad_mid_norm
    grad_mid_low = grad_mid.astype(jnp.bfloat16)
    grad_mid_pair = both_cores(grad_mid_low)
    out_grads, attended_pair = pair_back(
        grad_mid_pair, placed_attended, select_out, weight_out
    )
    grad_attended_low = pair_total(attended_pair).astype(jnp.bfloat16)

    out_arrived = [swap(g, m) for g, m in zip(out_grads[1:], out_plan.team[1:])]
    grad_query, grad_windows = attend_back(
        query_low, window_blocks, positions, prefix, log_total, attended_low, grad_attended_low
    )
    pair_parts = [grad_windows[-1]]
    for distance in range(1, window_span + 1):
        pair_parts.append(passed_along(grad_windows[window_span - distance], -distance))
    hidden_late, _ = tie(hidden_low, grad_query)
    out_blocks = block_products(hidden_late, weight_down, TEAM)
    out_total = out_blocks[0]
    for block, mask in zip(out_blocks[1:], masks[1:]):
        out_total = out_total + swap(block, mask).astype(jnp.float32)
    block_out = (mid_rows + out_total).astype(jnp.bfloat16)
    grad_projected = turn_back(grad_query, pair_parts, tables)
    in_grads, normed_grads = pair_back(
        both_cores(grad_projected), placed_one, select_in, weight_in
    )
    in_arrived = [swap(g, m) for g, m in zip(in_grads[1:], in_plan.team[1:])]
    pair_sent, down_sent, out_arrived, _ = tie(pair_sent, down_sent, out_arrived, in_grads[0])
    pair_sum = in_plan.outer_sum(pair_own, pair_sent)
    down_sum = in_plan.outer_sum(down_own, down_sent)
    grad_down = lax.ppermute(down_sum.astype(LINK), AXIS, trade_route).astype(jnp.float32).reshape(-1)
    pair_blocks_t = pair_sum.reshape(len(in_plan.team), in_plan.pitch, 2 * team_width)
    pair_low = pair_blocks_t.astype(LINK)
    returned = [
        swap(pick(pair_low, team_index ^ i), m) if m else pick(pair_low, team_index)
        for i, m in enumerate(in_plan.team)
    ]
    back_stack = jnp.stack(returned)[:, : in_plan.rows]
    natural = (back_stack[:, :, :team_width], back_stack[:, :, team_width:])

    def owned(grad_slabs):
        columns = []
        for t in range(TEAM):
            column_part = jnp.zeros_like(grad_slabs[0])
            for i, s in enumerate(member_shift):
                column_part = jnp.where((member ^ s) == t, grad_slabs[i], column_part)
            columns.append(column_part)
        return in_plan.own_share(
            jnp.concatenate(columns, axis=1).astype(jnp.float32), place
        )

    grad_gate = owned(natural[0])
    grad_up = owned(natural[1])

    def weight_share(plan, own, arrived_blocks):
        own, *blocks = reduce_split(own, arrived_blocks, 1 << len(plan.outer[-1]))
        return plan.outer_sum(own, plan.outer_send(blocks))[: plan.rows]

    out_share = weight_share(out_plan, out_grads[0], out_arrived)
    grad_out = out_plan.own_share(out_share, place)
    in_share = weight_share(in_plan, in_grads[0], in_arrived)
    grad_query_weight = in_plan.own_share(in_share[:, :q_width], place)
    grad_key_weight = in_plan.own_share(in_share[:, q_width : q_width + k_width], place)
    grad_value_weight = in_plan.own_share(in_share[:, q_width + k_width :], place)
    grad_normed_one = pair_total(normed_grads)
    grad_in_norm, grad_gain_one = norm_backward(input_rows, scale_one, norm1_gain, grad_normed_one)
    grad_in = (grad_mid + grad_in_norm).astype(jnp.bfloat16)
    gains = jnp.stack([grad_gain_one, grad_gain_two])
    for bit in range(device_count.bit_length() - 1):
        gains = gains + swap(gains, 1 << bit)
    return (
        block_out,
        grad_in,
        gains[0],
        grad_query_weight,
        grad_key_weight,
        grad_value_weight,
        grad_out,
        gains[1],
        grad_gate,
        grad_up,
        grad_down,
    )


def solution(mesh):
    placed = (
        P("fsdp", None),
        P("fsdp"),
        P(),
        P("fsdp"),
        P("fsdp"),
        P("fsdp"),
        P("fsdp"),
        P(),
        P("fsdp"),
        P("fsdp"),
        P("fsdp"),
        P("fsdp", None),
    )
    return jax.shard_map(
        local,
        mesh=mesh,
        in_specs=placed,
        out_specs=(
            P("fsdp", None),
            P("fsdp", None),
            P(),
            P("fsdp"),
            P("fsdp"),
            P("fsdp"),
            P("fsdp"),
            P(),
            P("fsdp"),
            P("fsdp"),
            P("fsdp"),
        ),
        check_vma=False,
    )
```

```python
import math

import jax
import jax.numpy as jnp
from jax import lax
from jax.experimental import pallas as pl
from jax.experimental.pallas import tpu as pltpu
from jax.sharding import PartitionSpec as P


KV_HEADS = 5
HEAD_DIM = 64
MAXLEN = 512


EPS = 1e-05
NEG_FILL = -1e30
AXIS = "fsdp"
TEAM_BITS = (1, 2)
TEAM = 1 << len(TEAM_BITS)
LOW_BITS = 3
ROW_TILE = 16
LINK = jnp.bfloat16
LANES = 128


def swap(block, mask):
    size = lax.axis_size(AXIS)
    return lax.ppermute(block, AXIS, [(i, i ^ mask) for i in range(size)])


def passed_along(block, distance):
    devices = range(lax.axis_size(AXIS))
    route = [(i - distance, i) for i in devices if i - distance in devices]
    return lax.ppermute(block, AXIS, route)


def pick(stack, index, axis=0):
    return lax.dynamic_index_in_dim(stack, index, axis, keepdims=False)


def team_masks():
    masks = []
    for member in range(TEAM):
        masks.append(sum(((member >> j) & 1) << bit for j, bit in enumerate(TEAM_BITS)))
    return masks


def rotary_tables(positions):
    half_width = HEAD_DIM // 2
    frequency = jnp.exp(
        jnp.arange(half_width, dtype=jnp.float32) * (-2.0 * math.log(10000.0) / HEAD_DIM)
    )
    angles = positions.astype(jnp.float32)[:, None] * frequency[None, :]
    repeats = LANES // half_width
    return (jnp.tile(jnp.cos(angles), (1, repeats)), jnp.tile(jnp.sin(angles), (1, repeats)))


def rotate(matrix, cosine, sine_table):
    half_width = HEAD_DIM // 2
    lane = lax.broadcasted_iota(jnp.int32, cosine.shape, 1)
    first_half = lane % HEAD_DIM < half_width
    signed = jnp.where(first_half, -sine_table, sine_table)
    turned = []
    for start in range(0, matrix.shape[1], LANES):
        part = matrix[:, start : start + LANES]
        other = jnp.where(
            first_half,
            pltpu.roll(part, LANES - half_width, 1),
            pltpu.roll(part, half_width, 1),
        )
        turned.append(part * cosine + other * signed)
    return jnp.concatenate(turned, axis=1)


def norm_scale(matrix):
    return lax.rsqrt(jnp.mean(matrix * matrix, axis=1, keepdims=True) + EPS)


def norm_backward(matrix, scale_rows, gain, grad_normed):
    unit_rows = matrix * scale_rows
    weighted = grad_normed * gain[None, :]
    grad_gain = jnp.sum(grad_normed * unit_rows, axis=0)
    grad_rows = scale_rows * (
        weighted - unit_rows * jnp.mean(weighted * unit_rows, axis=1, keepdims=True)
    )
    return (grad_rows, grad_gain)


def back_product(left_side, weight):
    return lax.dot_general(
        left_side, weight, (((1,), (1,)), ((), ())), preferred_element_type=jnp.float32
    )


def forward_product(left_side, weight):
    return jnp.dot(left_side, weight, preferred_element_type=jnp.float32)


def product(left_side, right_side, left_dim, right_dim):
    return lax.dot_general(
        left_side,
        right_side,
        (((left_dim,), (right_dim,)), ((), ())),
        preferred_element_type=jnp.float32,
    )


def kernel_call(body, outs, operands):
    return pl.pallas_call(
        body,
        out_shape=[jax.ShapeDtypeStruct(shape, dtype) for shape, dtype in outs],
        compiler_params=pltpu.CompilerParams(vmem_limit_bytes=60 * 1024 * 1024),
    )(*operands)


def tie(*values):
    return lax.optimization_barrier(values)


def bit_groups(bits):
    return [bits[i : i + 2] for i in range(0, len(bits), 2)]


def group_masks(bits):
    masks = [0]
    for bit in bits:
        masks += [m | (1 << bit) for m in masks]
    return masks


def spread(block, masks):
    return [block] + [swap(block, mask) for mask in masks[1:]]


def reduce_split(own, received, count):
    rows = own.shape[0] // count
    width = own.shape[1]

    def body(*refs):
        total = refs[0][...]
        for ref in refs[1 : 1 + len(received)]:
            total = total + ref[...].astype(jnp.float32)
        for i, out in enumerate(refs[1 + len(received) :]):
            out[...] = total[i * rows : (i + 1) * rows].astype(out.dtype)

    outs = [((rows, width), jnp.float32 if i == 0 else LINK) for i in range(count)]
    return kernel_call(body, outs, [own] + list(received))


def sum_columns(own, received, rows, widths):
    count = len(received)

    def body(*refs):
        start = 0
        for out, width in zip(refs[1 + count :], widths):
            total = refs[0][:rows, start : start + width]
            for ref in refs[1 : 1 + count]:
                total = total + ref[:rows, start : start + width].astype(jnp.float32)
            out[...] = total
            start += width

    outs = [((rows, width), jnp.float32) for width in widths]
    return kernel_call(body, outs, [own] + list(received))


class RowPlan:
    def __init__(self, row_total):
        size = lax.axis_size(AXIS)
        self.unit = size // math.gcd(size, row_total)
        self.rows = self.unit * row_total // size
        self.pitch = -(-self.rows // ROW_TILE) * ROW_TILE
        self.row_total = row_total
        unit_bits = self.unit.bit_length() - 1
        self.low = list(range(unit_bits))
        free = list(range(unit_bits, size.bit_length() - 1))
        self.outer = bit_groups([b for b in free if b >= LOW_BITS])
        self.team = group_masks([b for b in free if b in TEAM_BITS])
        self.last = group_masks([b for b in free if b < LOW_BITS and b not in TEAM_BITS])
        self.outer_set = group_masks([b for group in self.outer for b in group])

    def selector(self, base, distances):
        start = jnp.repeat(
            jnp.array([m // self.unit for m in distances], jnp.int32), self.pitch
        )
        within = jnp.tile(jnp.arange(self.pitch, dtype=jnp.int32), len(distances))
        row = ((base // self.unit) ^ start) * self.rows + within
        row = jnp.where(within < self.rows, row, -1)
        return (jnp.arange(self.row_total, dtype=jnp.int32)[:, None] == row[None, :]).astype(
            jnp.bfloat16
        )

    def whole_rows(self, flat, place):
        for bit in self.low:
            other = swap(flat, 1 << bit)
            high = (place >> bit) & 1
            flat = jnp.concatenate(
                [jnp.where(high == 1, other, flat), jnp.where(high == 1, flat, other)]
            )
        return flat.reshape(self.rows, -1)

    def own_share(self, block, place):
        flat = block.reshape(-1)
        for bit in reversed(self.low):
            high = (place >> bit) & 1
            halves = flat.reshape(2, -1)
            flat = pick(halves, high) + swap(
                pick(halves, 1 - high).astype(LINK), 1 << bit
            ).astype(jnp.float32)
        return flat

    def padded(self, block):
        return jnp.pad(block, ((0, self.pitch - self.rows), (0, 0)))

    def outer_pieces(self, block):
        pieces = [block]
        for group in self.outer:
            block = jnp.concatenate(pieces) if len(pieces) > 1 else pieces[0]
            pieces = spread(block, group_masks(group))
        return pieces

    def outer_send(self, blocks):
        return [swap(b, m) for b, m in zip(blocks, group_masks(self.outer[-1])[1:])]

    def outer_sum(self, own, arrived):
        for step, group in enumerate(reversed(self.outer)):
            following = self.outer[len(self.outer) - 2 - step] if step + 1 < len(self.outer) else []
            own, *blocks = reduce_split(own, arrived, 1 << len(following))
            arrived = [swap(b, m) for b, m in zip(blocks, group_masks(following)[1:])]
        return own


def pair_project(tokens, select, pieces):
    rows = tokens[0].shape[0]
    count = len(tokens)
    width = pieces[0].shape[1]
    depth = pieces[0].shape[0]

    def body(*refs):
        select_ref = refs[count]
        weights = refs[count + 1 : count + 1 + len(pieces)]
        outs = refs[count + 1 + len(pieces) :]
        tokens_all = jnp.concatenate([refs[i][...] for i in range(count)], axis=0)
        placed = product(tokens_all, select_ref[...], 1, 0).astype(jnp.bfloat16)
        outs[count][...] = placed
        total = product(placed[:, :depth], weights[0][...], 1, 0)
        for j in range(1, len(pieces)):
            total += product(placed[:, j * depth : (j + 1) * depth], weights[j][...], 1, 0)
        for i in range(count):
            outs[i][...] = total[i * rows : (i + 1) * rows]

    outs = [((rows, width), jnp.float32)] * count
    outs.append(((count * rows, select.shape[1]), jnp.bfloat16))
    results = kernel_call(body, outs, list(tokens) + [select] + list(pieces))
    return results[:count], results[count]


def pair_back(grads, placed, select, pieces):
    count = len(grads)
    rows = grads[0].shape[0]
    width = pieces[0].shape[1]
    depth = pieces[0].shape[0]
    features = select.shape[0]

    def body(*refs):
        placed_ref, select_ref = refs[count : count + 2]
        weights = refs[count + 2 : count + 2 + len(pieces)]
        outs = refs[count + 2 + len(pieces) :]
        grads_all = jnp.concatenate([refs[i][...] for i in range(count)], axis=0)
        total = None
        for j in range(len(pieces)):
            span = slice(j * depth, (j + 1) * depth)
            outs[j][...] = product(placed_ref[:, span], grads_all, 0, 0).astype(outs[j].dtype)
            back = product(grads_all, weights[j][...], 1, 1)
            high = back.astype(jnp.bfloat16)
            rest = (back - high.astype(jnp.float32)).astype(jnp.bfloat16)
            chosen = select_ref[:, span]
            part = product(high, chosen, 1, 1) + product(rest, chosen, 1, 1)
            total = part if total is None else total + part
        for i in range(count):
            outs[len(pieces) + i][...] = total[i * rows : (i + 1) * rows]

    outs = [((depth, width), jnp.float32 if j == 0 else LINK) for j in range(len(pieces))]
    outs += [((rows, features), jnp.float32)] * count
    results = kernel_call(body, outs, list(grads) + [placed, select] + list(pieces))
    return results[: len(pieces)], results[len(pieces) :]


def feed_forward(normed_blocks, cotangent_blocks, pair_pieces, down):
    count = len(normed_blocks)
    rows, features = normed_blocks[0].shape
    total_rows = count * rows
    depth, both = pair_pieces[0].shape
    width = both // 2
    pair_count = len(pair_pieces)

    def body(*refs):
        weights = refs[2 * count : 2 * count + pair_count]
        down_ref = refs[2 * count + pair_count]
        hidden_out, low_out, *back_outs = refs[2 * count + pair_count + 1 :]
        placed = jnp.concatenate([refs[i][...] for i in range(count)], axis=0)
        grads = jnp.concatenate([refs[count + i][...] for i in range(count)], axis=0)
        total = product(placed[:, :depth], weights[0][...], 1, 0)
        for j in range(1, pair_count):
            total += product(placed[:, j * depth : (j + 1) * depth], weights[j][...], 1, 0)
        gate_pre = total[:, :width]
        up_pre = total[:, width:]
        sigmoid_gate = 1.0 / (1.0 + jnp.exp(-gate_pre))
        silu_gate = gate_pre * sigmoid_gate
        hidden_out[...] = (silu_gate * up_pre).astype(jnp.bfloat16)
        grad_hidden = product(grads, down_ref[...], 1, 1)
        low_out[:, :width] = (
            grad_hidden * up_pre * sigmoid_gate * (1.0 + gate_pre * (1.0 - sigmoid_gate))
        ).astype(jnp.bfloat16)
        low_out[:, width:] = (grad_hidden * silu_gate).astype(jnp.bfloat16)
        low = low_out[...]
        for j in range(pair_count):
            back = product(low, weights[j][...], 1, 1)
            for i in range(count):
                part = back[i * rows : (i + 1) * rows]
                back_outs[i][:, j * depth : (j + 1) * depth] = part.astype(back_outs[i].dtype)

    outs = [((total_rows, width), jnp.bfloat16), ((total_rows, both), jnp.bfloat16)]
    outs += [((rows, features), jnp.float32 if i == 0 else LINK) for i in range(count)]
    operands = list(normed_blocks) + list(cotangent_blocks) + list(pair_pieces) + [down]
    results = kernel_call(body, outs, operands)
    return results[0], results[1], results[2:]


def split_products(left_blocks, right_side, first_rows):
    count = len(left_blocks)
    all_rows = left_blocks[0].shape[1]
    width = right_side.shape[1]

    def body(*refs):
        left = jnp.concatenate([refs[i][...] for i in range(count)], axis=0)
        right = refs[count][...]
        refs[count + 1][...] = product(left[:, :first_rows], right, 0, 0)
        if first_rows < all_rows:
            refs[count + 2][...] = product(left[:, first_rows:], right, 0, 0).astype(LINK)

    outs = [((first_rows, width), jnp.float32)]
    if first_rows < all_rows:
        outs.append(((all_rows - first_rows, width), LINK))
    return kernel_call(body, outs, list(left_blocks) + [right_side])


def turn(projected_parts, tables, q_width, k_width):
    rows = projected_parts[0].shape[0]
    count = len(projected_parts)

    def body(*refs):
        cosine_ref, sine_ref, query_out, pair_out = refs[count:]
        total = refs[0][...]
        for ref in refs[1:count]:
            total = total + ref[...]
        turned = rotate(total[:, : q_width + k_width], cosine_ref[...], sine_ref[...])
        query_out[...] = turned[:, :q_width].astype(jnp.bfloat16)
        pair_out[...] = jnp.concatenate(
            [turned[:, q_width:], total[:, q_width + k_width :]], axis=1
        ).astype(jnp.bfloat16)

    outs = [((rows, q_width), jnp.bfloat16), ((rows, 2 * k_width), jnp.bfloat16)]
    return kernel_call(body, outs, list(projected_parts) + list(tables))


def turn_back(grad_query, pair_parts, tables):
    rows, q_width = grad_query.shape
    k_width = pair_parts[0].shape[1] // 2

    def body(query_ref, cosine_ref, sine_ref, *refs):
        *parts, out = refs
        total = parts[0][...]
        for ref in parts[1:]:
            total = total + ref[...].astype(jnp.float32)
        heads = jnp.concatenate([query_ref[...], total[:, :k_width]], axis=1)
        turned = rotate(heads, cosine_ref[...], -sine_ref[...])
        out[...] = jnp.concatenate([turned, total[:, k_width:]], axis=1).astype(jnp.bfloat16)

    outs = [((rows, q_width + 2 * k_width), jnp.bfloat16)]
    return kernel_call(body, outs, [grad_query] + list(tables) + list(pair_parts))[0]


def allowed_pairs(position_ref, row_count, key_count, prefix):
    key_offset = lax.broadcasted_iota(jnp.int32, (row_count, key_count), 1) - prefix
    row_index = lax.broadcasted_iota(jnp.int32, (row_count, key_count), 0)
    return (key_offset <= row_index) & (key_offset >= row_index - position_ref[...])


def group_rows(ref, group, size):
    start = group * size * HEAD_DIM
    return jnp.concatenate(
        [ref[:, start + h * HEAD_DIM : start + (h + 1) * HEAD_DIM] for h in range(size)], axis=0
    )


def side_by_side(stacked, row_count):
    return [stacked[h * row_count : (h + 1) * row_count] for h in range(stacked.shape[0] // row_count)]


def attend(query_block, window_blocks, position_block, prefix):
    row_count, q_width = query_block.shape
    k_width = window_blocks[0].shape[1] // 2
    key_count = len(window_blocks) * row_count
    group_size = q_width // k_width

    def body(query_ref, position_ref, *refs):
        *window_refs, out_ref, log_ref = refs
        window = jnp.concatenate([ref[...] for ref in window_refs], axis=0)
        allowed = allowed_pairs(position_ref, row_count, key_count, prefix)
        fill = jnp.where(allowed, 0.0, NEG_FILL)
        fill = jnp.concatenate([fill] * group_size, axis=0)
        columns = []
        for g in range(KV_HEADS):
            span = slice(g * HEAD_DIM, (g + 1) * HEAD_DIM)
            scores = product(group_rows(query_ref, g, group_size), window[:, span], 1, 1)
            scores = jnp.where(fill < 0.0, NEG_FILL, scores * HEAD_DIM ** (-0.5))
            row_max = jnp.max(scores, axis=1, keepdims=True)
            total = jnp.sum(jnp.exp(scores - row_max), axis=1, keepdims=True)
            log_total = row_max + jnp.log(total)
            log_ref[g] = log_total
            prob_low = jnp.exp(scores - log_total).astype(jnp.bfloat16)
            values = window[:, k_width + g * HEAD_DIM : k_width + (g + 1) * HEAD_DIM]
            columns += side_by_side(product(prob_low, values, 1, 0), row_count)
        out_ref[...] = jnp.concatenate(columns, axis=1).astype(jnp.bfloat16)

    outs = [
        ((row_count, q_width), jnp.bfloat16),
        ((KV_HEADS, group_size * row_count, 1), jnp.float32),
    ]
    operands = [query_block, position_block[:, None]] + list(window_blocks)
    return kernel_call(body, outs, operands)


def attend_back(
    query_block, window_blocks, position_block, prefix, log_total, attended_block, grad_block
):
    row_count, q_width = query_block.shape
    k_width = window_blocks[0].shape[1] // 2
    count = len(window_blocks)
    key_count = count * row_count
    group_size = q_width // k_width

    def body(query_ref, position_ref, log_ref, attended_ref, grad_ref, *refs):
        window_refs = refs[:count]
        query_out, *window_outs = refs[count:]
        window = jnp.concatenate([ref[...] for ref in window_refs], axis=0)
        allowed = allowed_pairs(position_ref, row_count, key_count, prefix)
        fill = jnp.where(allowed, 0.0, NEG_FILL)
        fill = jnp.concatenate([fill] * group_size, axis=0)
        query_columns = []
        key_columns = []
        value_columns = []
        for g in range(KV_HEADS):
            span = slice(g * HEAD_DIM, (g + 1) * HEAD_DIM)
            keys = window[:, span]
            values = window[:, k_width + g * HEAD_DIM : k_width + (g + 1) * HEAD_DIM]
            queries = group_rows(query_ref, g, group_size)
            grads = group_rows(grad_ref, g, group_size)
            outputs = group_rows(attended_ref, g, group_size)
            scores = product(queries, keys, 1, 1)
            scores = jnp.where(fill < 0.0, NEG_FILL, scores * HEAD_DIM ** (-0.5))
            prob_full = jnp.exp(scores - log_ref[g])
            grad_prob = product(grads, values, 1, 1)
            delta_sum = jnp.sum(
                grads.astype(jnp.float32) * outputs.astype(jnp.float32), axis=1, keepdims=True
            )
            grad_score = (prob_full * (grad_prob - delta_sum) * HEAD_DIM ** (-0.5)).astype(
                jnp.bfloat16
            )
            query_columns += side_by_side(product(grad_score, keys, 1, 0), row_count)
            key_columns.append(product(grad_score, queries, 0, 0))
            value_columns.append(product(prob_full.astype(jnp.bfloat16), grads, 0, 0))
        query_out[...] = jnp.concatenate(query_columns, axis=1)
        total = jnp.concatenate(key_columns + value_columns, axis=1)
        for i, out in enumerate(window_outs):
            out[...] = total[i * row_count : (i + 1) * row_count].astype(out.dtype)

    outs = [((row_count, q_width), jnp.float32)]
    outs += [
        ((row_count, 2 * k_width), jnp.float32 if i == count - 1 else LINK) for i in range(count)
    ]
    operands = [query_block, position_block[:, None], log_total, attended_block, grad_block]
    results = kernel_call(body, outs, operands + list(window_blocks))
    return results[0], results[1:]


def starts_call(body, outs, starts, operands, scratch=()):
    return pl.pallas_call(
        body,
        out_shape=[jax.ShapeDtypeStruct(shape, dtype) for shape, dtype in outs],
        in_specs=[pl.BlockSpec(memory_space=pltpu.SMEM)]
        + [pl.BlockSpec(memory_space=pltpu.VMEM)] * len(operands),
        scratch_shapes=list(scratch),
        compiler_params=pltpu.CompilerParams(vmem_limit_bytes=60 * 1024 * 1024),
    )(starts, *operands)


def arrange_rows(pieces, starts, chunk, order):
    total = sum(piece.shape[0] for piece in pieces)
    width = pieces[0].shape[1]
    if chunk % ROW_TILE:
        stacked = jnp.concatenate(pieces)
        return forward_product(order, stacked).astype(jnp.bfloat16)
    per_piece = pieces[0].shape[0] // chunk

    def body(starts_ref, *refs):
        for j in range(total // chunk):
            at = pl.multiple_of(starts_ref[j], ROW_TILE)
            start = (j % per_piece) * chunk
            refs[-1][pl.ds(at, chunk), :] = refs[j // per_piece][start : start + chunk, :]

    return starts_call(body, [((total, width), jnp.bfloat16)], starts, list(pieces))[0]


def down_products(hidden, grads, starts, chunk, order):
    if chunk % ROW_TILE:
        placed = forward_product(hidden, order).astype(jnp.bfloat16)
        return split_products([placed], jnp.concatenate(grads), hidden.shape[1] // 2)
    half = hidden.shape[1] // 2
    width = grads[0].shape[1]
    count = len(grads)

    def body(starts_ref, *refs):
        hidden_ref = refs[0]
        own, other, total_ref = refs[1 + count :]
        right = jnp.concatenate([refs[1 + i][...] for i in range(count)], axis=0)
        total_ref[...] = product(hidden_ref[...], right, 0, 0)
        for j in range(2 * half // chunk):
            rows = total_ref[pl.ds(pl.multiple_of(starts_ref[j], ROW_TILE), chunk), :]
            target = own if j * chunk < half else other
            start = j * chunk % half
            target[start : start + chunk, :] = rows.astype(target.dtype)

    outs = [((half, width), jnp.float32), ((half, width), LINK)]
    scratch = [pltpu.VMEM((2 * half, width), jnp.float32)]
    return starts_call(body, outs, starts, [hidden] + list(grads), scratch)


def block_products(left_side, down, count):
    rows = left_side.shape[0] // count
    width = down.shape[1]

    def body(left_ref, down_ref, *outs):
        total = product(left_ref[...], down_ref[...], 1, 0)
        for i, out in enumerate(outs):
            out[...] = total[i * rows : (i + 1) * rows].astype(out.dtype)

    outs = [((rows, width), jnp.float32 if i == 0 else LINK) for i in range(count)]
    return kernel_call(body, outs, [left_side, down])


def local(
    hidden_in,
    positions,
    norm1_gain,
    q_weight,
    k_weight,
    v_weight,
    o_weight,
    norm2_gain,
    gate_weight,
    up_weight,
    down_weight,
    cotangent,
):
    tok_rows = hidden_in.shape[0]
    model_width = hidden_in.shape[1]
    device_count = lax.axis_size(AXIS)
    place = lax.axis_index(AXIS)
    member = (place >> TEAM_BITS[0]) & (TEAM - 1)
    outer_index = place >> LOW_BITS
    core = place & 1
    outer_bits = device_count.bit_length() - 1 - LOW_BITS
    top_shift = outer_bits - len(TEAM_BITS)
    window_span = (MAXLEN + tok_rows - 2) // tok_rows
    prefix = window_span * tok_rows
    q_width = q_weight.shape[0] * device_count // model_width
    k_width = k_weight.shape[0] * device_count // model_width
    ff_width = gate_weight.shape[0] * device_count // model_width
    team_width = ff_width // TEAM
    down_rows = ff_width // device_count
    masks = team_masks()

    in_plan = RowPlan(model_width)
    out_plan = RowPlan(q_width)
    paired = len(in_plan.last) > 1

    def both_cores(block):
        return [block, swap(block, 1)] if paired else [block]

    def pair_total(outs):
        return outs[0] + swap(outs[1], 1) if paired else outs[0]

    def distances(plan):
        return [t ^ o for t in plan.team for o in plan.outer_set]

    input_rows = hidden_in.astype(jnp.float32)
    scale_one = norm_scale(input_rows)
    normed_one = (input_rows * scale_one * norm1_gain[None, :]).astype(jnp.bfloat16)
    normed_pair = both_cores(normed_one)

    in_block = in_plan.padded(
        jnp.concatenate([in_plan.whole_rows(w, place) for w in (q_weight, k_weight, v_weight)], 1)
    )
    in_outer = jnp.concatenate(in_plan.outer_pieces(in_block))
    select_in = in_plan.selector(place, distances(in_plan))
    select_out = out_plan.selector(place, distances(out_plan))

    def traded(i):
        outer, mem, c = i >> LOW_BITS, (i >> TEAM_BITS[0]) & (TEAM - 1), i & 1
        inner = outer & ((1 << top_shift) - 1)
        return (((mem << top_shift) | inner) << LOW_BITS) | ((outer >> top_shift) << TEAM_BITS[0]) | c

    trade_route = [(i, traded(i)) for i in range(device_count)]
    chunk_start = []
    for c in range(2):
        for o in in_plan.outer_set:
            o_from = outer_index ^ (o >> LOW_BITS)
            inner = o_from & ((1 << top_shift) - 1)
            chunk = (inner << LOW_BITS) | ((o_from >> top_shift) << TEAM_BITS[0]) | (core ^ c)
            chunk_start.append(chunk * down_rows)
    column = jnp.repeat(jnp.stack(chunk_start), down_rows) + jnp.tile(
        jnp.arange(down_rows, dtype=jnp.int32), len(chunk_start)
    )
    unit_starts = jnp.stack(chunk_start).astype(jnp.int32)
    select_unit = (
        jnp.arange(team_width, dtype=jnp.int32)[:, None] == column[None, :]
    ).astype(jnp.bfloat16)

    def slabs(flat):
        whole = in_plan.whole_rows(flat, place)
        parts = jnp.concatenate(
            [whole[:, t * team_width : (t + 1) * team_width] for t in range(TEAM)]
        )
        return parts.reshape(TEAM, -1, team_width)

    gap = in_plan.pitch - in_plan.rows
    pair_slabs = jnp.pad(
        jnp.concatenate([slabs(gate_weight), slabs(up_weight)], axis=2), ((0, 0), (0, gap), (0, 0))
    )
    member_shift = [m >> TEAM_BITS[0] for m in in_plan.team]
    arrived = [
        swap(pick(pair_slabs, member ^ s), m) if m else pick(pair_slabs, member)
        for s, m in zip(member_shift, in_plan.team)
    ]
    team_index = sum(
        ((place >> (m.bit_length() - 1)) & 1) << i
        for i, m in enumerate(m for m in in_plan.team if m & (m - 1) == 0 and m)
    )
    arrived = jnp.stack(arrived)
    pair_block = jnp.concatenate(
        [pick(arrived, team_index ^ i) for i in range(len(in_plan.team))]
    )
    down_block = lax.ppermute(down_weight.reshape(down_rows, model_width), AXIS, trade_route)
    _, pair_block, down_block, o_flat = tie(in_outer, pair_block, down_block, o_weight)
    weight_in = spread(in_outer, in_plan.team)
    out_pieces = out_plan.outer_pieces(out_plan.padded(out_plan.whole_rows(o_flat, place)))
    pair_outer = in_plan.outer_pieces(pair_block)
    down_outer = in_plan.outer_pieces(down_block)
    out_outer = jnp.concatenate(out_pieces)
    weight_pair = pair_outer + [swap(p, m) for m in in_plan.last[1:] for p in pair_outer]
    ff_distances = [c ^ o ^ t for c in in_plan.last for o in in_plan.outer_set for t in in_plan.team]
    select_ff = in_plan.selector(place & ~in_plan.team[-1], ff_distances)
    weight_down = arrange_rows(
        down_outer + [swap(piece, 1) for piece in down_outer], unit_starts, down_rows, select_unit
    )

    tables = rotary_tables(positions)
    projected_pair, placed_one = pair_project(normed_pair, select_in, weight_in)
    projected_parts = list(projected_pair[:1]) + [swap(part, 1) for part in projected_pair[1:]]
    out_outer, cotangent_late, _ = tie(out_outer, cotangent, projected_parts)
    weight_out = spread(out_outer, out_plan.team)
    query_low, key_value = turn(projected_parts, tables, q_width, k_width)
    pieces = [passed_along(key_value, d) for d in range(window_span, 0, -1)]
    cotangent_blocks = spread(cotangent_late, masks)
    window_blocks = pieces + [key_value]
    attended_low, log_total = attend(query_low, window_blocks, positions, prefix)
    mixed_pair, placed_attended = pair_project(both_cores(attended_low), select_out, weight_out)
    mid_rows = input_rows + pair_total(mixed_pair)
    scale_two = norm_scale(mid_rows)
    normed_two = (mid_rows * scale_two * norm2_gain[None, :]).astype(jnp.bfloat16)

    placed_two = forward_product(normed_two, select_ff).astype(jnp.bfloat16)
    normed_blocks = spread(placed_two, masks)
    hidden_low, grad_low, back_blocks = feed_forward(
        normed_blocks, cotangent_blocks, weight_pair, weight_down
    )
    back_arrived = [swap(block, mask) for block, mask in zip(back_blocks[1:], masks[1:])]
    back_total = back_blocks[0]
    for block in back_arrived:
        back_total = back_total + block.astype(jnp.float32)
    back_high = lax.reduce_precision(back_total, 8, 7)
    grad_normed_two = back_product(back_high.astype(jnp.bfloat16), select_ff) + back_product(
        (back_total - back_high).astype(jnp.bfloat16), select_ff
    )

    pair_rows = placed_two.shape[1] // len(in_plan.last)
    pair_grads = split_products(normed_blocks, grad_low, pair_rows)
    pair_arrived = [swap(g, m) for g, m in zip(pair_grads[1:], in_plan.last[1:])]
    down_grads = down_products(hidden_low, cotangent_blocks, unit_starts, down_rows, select_unit)
    down_arrived = [swap(down_grads[1], 1)]
    outer_group = 1 << len(in_plan.outer[-1])
    pair_own, *pair_blocks = reduce_split(pair_grads[0], pair_arrived, outer_group)
    down_own, *down_blocks = reduce_split(down_grads[0], down_arrived, outer_group)
    pair_sent = in_plan.outer_send(pair_blocks)
    down_sent = in_plan.outer_send(down_blocks)
    grad_mid_norm, grad_gain_two = norm_backward(mid_rows, scale_two, norm2_gain, grad_normed_two)
    grad_mid = cotangent.astype(jnp.float32) + grad_mid_norm
    grad_mid_low = grad_mid.astype(jnp.bfloat16)
    grad_mid_pair = both_cores(grad_mid_low)
    out_grads, attended_pair = pair_back(
        grad_mid_pair, placed_attended, select_out, weight_out
    )
    grad_attended_low = pair_total(attended_pair).astype(jnp.bfloat16)

    out_arrived = [swap(g, m) for g, m in zip(out_grads[1:], out_plan.team[1:])]
    grad_query, grad_windows = attend_back(
        query_low, window_blocks, positions, prefix, log_total, attended_low, grad_attended_low
    )
    pair_parts = [grad_windows[-1]]
    for distance in range(1, window_span + 1):
        pair_parts.append(passed_along(grad_windows[window_span - distance], -distance))
    hidden_late, _ = tie(hidden_low, grad_query)
    out_blocks = block_products(hidden_late, weight_down, TEAM)
    out_swapped = [swap(block, mask) for block, mask in zip(out_blocks[1:], masks[1:])]
    out_total = out_blocks[0]
    for block in out_swapped:
        out_total = out_total + block.astype(jnp.float32)
    block_out = (mid_rows + out_total).astype(jnp.bfloat16)
    grad_projected = turn_back(grad_query, pair_parts, tables)
    grad_projected_pair = both_cores(grad_projected)
    in_grads, normed_grads = pair_back(grad_projected_pair, placed_one, select_in, weight_in)
    in_arrived = [swap(g, m) for g, m in zip(in_grads[1:], in_plan.team[1:])]
    pair_sent, down_sent, _ = tie(pair_sent, down_sent, in_grads[0])
    out_arrived, _ = tie(out_arrived, in_grads[0])
    pair_sum = in_plan.outer_sum(pair_own, pair_sent)
    down_sum = in_plan.outer_sum(down_own, down_sent)
    grad_down = lax.ppermute(down_sum.astype(LINK), AXIS, trade_route).astype(jnp.float32).reshape(-1)
    pair_blocks_t = pair_sum.reshape(len(in_plan.team), in_plan.pitch, 2 * team_width)
    pair_low = pair_blocks_t.astype(LINK)
    returned = [
        swap(pick(pair_low, team_index ^ i), m) if m else pick(pair_low, team_index)
        for i, m in enumerate(in_plan.team)
    ]
    back_stack = jnp.stack(returned)[:, : in_plan.rows]
    natural = (back_stack[:, :, :team_width], back_stack[:, :, team_width:])

    def owned(grad_slabs):
        columns = []
        for t in range(TEAM):
            column_part = jnp.zeros_like(grad_slabs[0])
            for i, s in enumerate(member_shift):
                column_part = jnp.where((member ^ s) == t, grad_slabs[i], column_part)
            columns.append(column_part)
        return in_plan.own_share(
            jnp.concatenate(columns, axis=1).astype(jnp.float32), place
        )

    grad_gate = owned(natural[0])
    grad_up = owned(natural[1])

    def team_share(plan, own, arrived_blocks):
        own, *blocks = reduce_split(own, arrived_blocks, 1 << len(plan.outer[-1]))
        return own, blocks

    out_own, out_split = team_share(out_plan, out_grads[0], out_arrived)
    out_sent = out_plan.outer_send(out_split)
    in_own, in_split = team_share(in_plan, in_grads[0], in_arrived)
    in_sent = in_plan.outer_send(in_split)
    out_share = out_plan.outer_sum(out_own, out_sent)[: out_plan.rows]
    grad_out = out_plan.own_share(out_share, place)
    if len(in_plan.outer) == 1:
        in_shares = sum_columns(in_own, in_sent, in_plan.rows, (q_width, k_width, k_width))
    else:
        in_share = in_plan.outer_sum(in_own, in_sent)[: in_plan.rows]
        in_shares = jnp.split(in_share, [q_width, q_width + k_width], axis=1)
    grad_query_weight, grad_key_weight, grad_value_weight = (
        in_plan.own_share(share, place) for share in in_shares
    )
    grad_normed_one = pair_total(normed_grads)
    grad_in_norm, grad_gain_one = norm_backward(input_rows, scale_one, norm1_gain, grad_normed_one)
    grad_in = (grad_mid + grad_in_norm).astype(jnp.bfloat16)
    gains = jnp.stack([grad_gain_one, grad_gain_two])
    for bit in range(device_count.bit_length() - 1):
        gains = reduce_split(gains, [swap(gains, 1 << bit)], 1)[0]
    return (
        block_out,
        grad_in,
        gains[0],
        grad_query_weight,
        grad_key_weight,
        grad_value_weight,
        grad_out,
        gains[1],
        grad_gate,
        grad_up,
        grad_down,
    )


def solution(mesh):
    placed = (
        P("fsdp", None),
        P("fsdp"),
        P(),
        P("fsdp"),
        P("fsdp"),
        P("fsdp"),
        P("fsdp"),
        P(),
        P("fsdp"),
        P("fsdp"),
        P("fsdp"),
        P("fsdp", None),
    )
    return jax.shard_map(
        local,
        mesh=mesh,
        in_specs=placed,
        out_specs=(
            P("fsdp", None),
            P("fsdp", None),
            P(),
            P("fsdp"),
            P("fsdp"),
            P("fsdp"),
            P("fsdp"),
            P(),
            P("fsdp"),
            P("fsdp"),
            P("fsdp"),
        ),
        check_vma=False,
    )
```

```python
import math

import jax
import jax.numpy as jnp
from jax import lax
from jax.experimental import pallas as pl
from jax.experimental.pallas import tpu as pltpu
from jax.sharding import PartitionSpec as P


KV_HEADS = 5
HEAD_DIM = 64
MAXLEN = 512


EPS = 1e-05
NEG_FILL = -1e30
AXIS = "fsdp"
TEAM_BITS = (1, 2)
TEAM = 1 << len(TEAM_BITS)
LOW_BITS = 3
ROW_TILE = 16
LINK = jnp.bfloat16
LANES = 128


def swap(block, mask):
    size = lax.axis_size(AXIS)
    return lax.ppermute(block, AXIS, [(i, i ^ mask) for i in range(size)])


def passed_along(block, distance):
    devices = range(lax.axis_size(AXIS))
    route = [(i - distance, i) for i in devices if i - distance in devices]
    return lax.ppermute(block, AXIS, route)


def pick(stack, index, axis=0):
    return lax.dynamic_index_in_dim(stack, index, axis, keepdims=False)


def team_masks():
    masks = []
    for member in range(TEAM):
        masks.append(sum(((member >> j) & 1) << bit for j, bit in enumerate(TEAM_BITS)))
    return masks


def rotary_tables(positions):
    half_width = HEAD_DIM // 2
    frequency = jnp.exp(
        jnp.arange(half_width, dtype=jnp.float32) * (-2.0 * math.log(10000.0) / HEAD_DIM)
    )
    angles = positions.astype(jnp.float32)[:, None] * frequency[None, :]
    repeats = LANES // half_width
    return (jnp.tile(jnp.cos(angles), (1, repeats)), jnp.tile(jnp.sin(angles), (1, repeats)))


def rotate(matrix, cosine, sine_table):
    half_width = HEAD_DIM // 2
    lane = lax.broadcasted_iota(jnp.int32, cosine.shape, 1)
    first_half = lane % HEAD_DIM < half_width
    signed = jnp.where(first_half, -sine_table, sine_table)
    turned = []
    for start in range(0, matrix.shape[1], LANES):
        part = matrix[:, start : start + LANES]
        other = jnp.where(
            first_half,
            pltpu.roll(part, LANES - half_width, 1),
            pltpu.roll(part, half_width, 1),
        )
        turned.append(part * cosine + other * signed)
    return jnp.concatenate(turned, axis=1)


def norm_scale(matrix):
    return lax.rsqrt(jnp.mean(matrix * matrix, axis=1, keepdims=True) + EPS)


def norm_backward(matrix, scale_rows, gain, grad_normed):
    unit_rows = matrix * scale_rows
    weighted = grad_normed * gain[None, :]
    grad_gain = jnp.sum(grad_normed * unit_rows, axis=0)
    grad_rows = scale_rows * (
        weighted - unit_rows * jnp.mean(weighted * unit_rows, axis=1, keepdims=True)
    )
    return (grad_rows, grad_gain)


def back_product(left_side, weight):
    return lax.dot_general(
        left_side, weight, (((1,), (1,)), ((), ())), preferred_element_type=jnp.float32
    )


def forward_product(left_side, weight):
    return jnp.dot(left_side, weight, preferred_element_type=jnp.float32)


def product(left_side, right_side, left_dim, right_dim):
    return lax.dot_general(
        left_side,
        right_side,
        (((left_dim,), (right_dim,)), ((), ())),
        preferred_element_type=jnp.float32,
    )


def kernel_call(body, outs, operands, scratch=()):
    return pl.pallas_call(
        body,
        scratch_shapes=list(scratch),
        out_shape=[jax.ShapeDtypeStruct(shape, dtype) for shape, dtype in outs],
        compiler_params=pltpu.CompilerParams(vmem_limit_bytes=60 * 1024 * 1024),
    )(*operands)


def tie(*values):
    return lax.optimization_barrier(values)


def bit_groups(bits):
    return [bits[i : i + 2] for i in range(0, len(bits), 2)]


def group_masks(bits):
    masks = [0]
    for bit in bits:
        masks += [m | (1 << bit) for m in masks]
    return masks


def spread(block, masks):
    return [block] + [swap(block, mask) for mask in masks[1:]]


def reduce_split(own, received, count):
    rows = own.shape[0] // count
    width = own.shape[1]

    def body(*refs):
        total = refs[0][...]
        for ref in refs[1 : 1 + len(received)]:
            total = total + ref[...].astype(jnp.float32)
        for i, out in enumerate(refs[1 + len(received) :]):
            out[...] = total[i * rows : (i + 1) * rows].astype(out.dtype)

    outs = [((rows, width), jnp.float32 if i == 0 else LINK) for i in range(count)]
    return kernel_call(body, outs, [own] + list(received))


def sum_columns(own, received, rows, widths):
    count = len(received)

    def body(*refs):
        start = 0
        for out, width in zip(refs[1 + count :], widths):
            total = refs[0][:rows, start : start + width]
            for ref in refs[1 : 1 + count]:
                total = total + ref[:rows, start : start + width].astype(jnp.float32)
            out[...] = total
            start += width

    outs = [((rows, width), jnp.float32) for width in widths]
    return kernel_call(body, outs, [own] + list(received))


class RowPlan:
    def __init__(self, row_total):
        size = lax.axis_size(AXIS)
        self.unit = size // math.gcd(size, row_total)
        self.rows = self.unit * row_total // size
        self.pitch = -(-self.rows // ROW_TILE) * ROW_TILE
        self.row_total = row_total
        unit_bits = self.unit.bit_length() - 1
        self.low = list(range(unit_bits))
        free = list(range(unit_bits, size.bit_length() - 1))
        self.outer = bit_groups([b for b in free if b >= LOW_BITS])
        self.team = group_masks([b for b in free if b in TEAM_BITS])
        self.last = group_masks([b for b in free if b < LOW_BITS and b not in TEAM_BITS])
        self.outer_set = group_masks([b for group in self.outer for b in group])

    def selector(self, base, distances):
        start = jnp.repeat(
            jnp.array([m // self.unit for m in distances], jnp.int32), self.pitch
        )
        within = jnp.tile(jnp.arange(self.pitch, dtype=jnp.int32), len(distances))
        row = ((base // self.unit) ^ start) * self.rows + within
        row = jnp.where(within < self.rows, row, -1)
        return (jnp.arange(self.row_total, dtype=jnp.int32)[:, None] == row[None, :]).astype(
            jnp.bfloat16
        )

    def whole_rows(self, flat, place):
        for bit in self.low:
            other = swap(flat, 1 << bit)
            high = (place >> bit) & 1
            flat = jnp.concatenate(
                [jnp.where(high == 1, other, flat), jnp.where(high == 1, flat, other)]
            )
        return flat.reshape(self.rows, -1)

    def own_share(self, block, place):
        flat = block.reshape(-1)
        for bit in reversed(self.low):
            high = (place >> bit) & 1
            halves = flat.reshape(2, -1)
            flat = pick(halves, high) + swap(
                pick(halves, 1 - high).astype(LINK), 1 << bit
            ).astype(jnp.float32)
        return flat

    def padded(self, block):
        return jnp.pad(block, ((0, self.pitch - self.rows), (0, 0)))

    def outer_pieces(self, block):
        pieces = [block]
        for group in self.outer:
            block = jnp.concatenate(pieces) if len(pieces) > 1 else pieces[0]
            pieces = spread(block, group_masks(group))
        return pieces

    def outer_send(self, blocks):
        return [swap(b, m) for b, m in zip(blocks, group_masks(self.outer[-1])[1:])]

    def outer_sum(self, own, arrived):
        for step, group in enumerate(reversed(self.outer)):
            following = self.outer[len(self.outer) - 2 - step] if step + 1 < len(self.outer) else []
            own, *blocks = reduce_split(own, arrived, 1 << len(following))
            arrived = [swap(b, m) for b, m in zip(blocks, group_masks(following)[1:])]
        return own


def pair_project(tokens, select, pieces):
    rows = tokens[0].shape[0]
    count = len(tokens)
    width = pieces[0].shape[1]

    def body(*refs):
        select_ref = refs[count]
        weights = refs[count + 1 : count + 1 + len(pieces)]
        outs = refs[count + 1 + len(pieces) :]
        tokens_all = jnp.concatenate([refs[i][...] for i in range(count)], axis=0)
        placed = product(tokens_all, select_ref[...], 1, 0).astype(jnp.bfloat16)
        outs[count][...] = placed
        total = product(placed, jnp.concatenate([w[...] for w in weights], axis=0), 1, 0)
        for i in range(count):
            outs[i][...] = total[i * rows : (i + 1) * rows]

    outs = [((rows, width), jnp.float32)] * count
    outs.append(((count * rows, select.shape[1]), jnp.bfloat16))
    results = kernel_call(body, outs, list(tokens) + [select] + list(pieces))
    return results[:count], results[count]


def pair_back(grads, placed, select, pieces):
    count = len(grads)
    rows = grads[0].shape[0]
    width = pieces[0].shape[1]
    depth = pieces[0].shape[0]
    features = select.shape[0]

    def body(*refs):
        placed_ref, select_ref = refs[count : count + 2]
        weights = refs[count + 2 : count + 2 + len(pieces)]
        outs = refs[count + 2 + len(pieces) :]
        grads_all = jnp.concatenate([refs[i][...] for i in range(count)], axis=0)
        grad_rows = product(placed_ref[...], grads_all, 0, 0)
        for j in range(len(pieces)):
            outs[j][...] = grad_rows[j * depth : (j + 1) * depth].astype(outs[j].dtype)
        back = product(grads_all, jnp.concatenate([w[...] for w in weights], axis=0), 1, 1)
        high = back.astype(jnp.bfloat16)
        rest = (back - high.astype(jnp.float32)).astype(jnp.bfloat16)
        both = product(jnp.concatenate([high, rest], axis=0), select_ref[...], 1, 1)
        total = both[: count * rows] + both[count * rows :]
        for i in range(count):
            outs[len(pieces) + i][...] = total[i * rows : (i + 1) * rows]

    outs = [((depth, width), jnp.float32 if j == 0 else LINK) for j in range(len(pieces))]
    outs += [((rows, features), jnp.float32)] * count
    results = kernel_call(body, outs, list(grads) + [placed, select] + list(pieces))
    return results[: len(pieces)], results[len(pieces) :]


def feed_forward(normed_blocks, cotangent_blocks, pair_pieces, down):
    count = len(normed_blocks)
    rows, features = normed_blocks[0].shape
    total_rows = count * rows
    both = pair_pieces[0].shape[1]
    width = both // 2
    pair_count = len(pair_pieces)

    def body(*refs):
        weights = refs[2 * count : 2 * count + pair_count]
        down_ref = refs[2 * count + pair_count]
        hidden_out, low_out, *back_outs = refs[2 * count + pair_count + 1 :]
        placed = jnp.concatenate([refs[i][...] for i in range(count)], axis=0)
        grads = jnp.concatenate([refs[count + i][...] for i in range(count)], axis=0)
        whole = jnp.concatenate([w[...] for w in weights], axis=0)
        total = product(placed, whole, 1, 0)
        gate_pre = total[:, :width]
        up_pre = total[:, width:]
        sigmoid_gate = 1.0 / (1.0 + jnp.exp(-gate_pre))
        silu_gate = gate_pre * sigmoid_gate
        hidden_out[...] = (silu_gate * up_pre).astype(jnp.bfloat16)
        grad_hidden = product(grads, down_ref[...], 1, 1)
        low_out[:, :width] = (
            grad_hidden * up_pre * sigmoid_gate * (1.0 + gate_pre * (1.0 - sigmoid_gate))
        ).astype(jnp.bfloat16)
        low_out[:, width:] = (grad_hidden * silu_gate).astype(jnp.bfloat16)
        low = low_out[...]
        back = product(low, whole, 1, 1)
        for i in range(count):
            back_outs[i][...] = back[i * rows : (i + 1) * rows].astype(back_outs[i].dtype)

    outs = [((total_rows, width), jnp.bfloat16), ((total_rows, both), jnp.bfloat16)]
    outs += [((rows, features), jnp.float32 if i == 0 else LINK) for i in range(count)]
    operands = list(normed_blocks) + list(cotangent_blocks) + list(pair_pieces) + [down]
    results = kernel_call(body, outs, operands)
    return results[0], results[1], results[2:]


def split_products(left_blocks, right_side, first_rows):
    count = len(left_blocks)
    all_rows = left_blocks[0].shape[1]
    width = right_side.shape[1]

    def body(*refs):
        left = jnp.concatenate([refs[i][...] for i in range(count)], axis=0)
        right = refs[count][...]
        refs[count + 1][...] = product(left[:, :first_rows], right, 0, 0)
        if first_rows < all_rows:
            refs[count + 2][...] = product(left[:, first_rows:], right, 0, 0).astype(LINK)

    outs = [((first_rows, width), jnp.float32)]
    if first_rows < all_rows:
        outs.append(((all_rows - first_rows, width), LINK))
    return kernel_call(body, outs, list(left_blocks) + [right_side])


def turn(projected_parts, tables, q_width, k_width):
    rows = projected_parts[0].shape[0]
    count = len(projected_parts)

    def body(*refs):
        cosine_ref, sine_ref, query_out, pair_out = refs[count:]
        total = refs[0][...]
        for ref in refs[1:count]:
            total = total + ref[...]
        turned = rotate(total[:, : q_width + k_width], cosine_ref[...], sine_ref[...])
        query_out[...] = turned[:, :q_width].astype(jnp.bfloat16)
        pair_out[...] = jnp.concatenate(
            [turned[:, q_width:], total[:, q_width + k_width :]], axis=1
        ).astype(jnp.bfloat16)

    outs = [((rows, q_width), jnp.bfloat16), ((rows, 2 * k_width), jnp.bfloat16)]
    return kernel_call(body, outs, list(projected_parts) + list(tables))


def turn_back(grad_query, pair_parts, tables):
    rows, q_width = grad_query.shape
    k_width = pair_parts[0].shape[1] // 2

    def body(query_ref, cosine_ref, sine_ref, *refs):
        *parts, out = refs
        total = parts[0][...]
        for ref in parts[1:]:
            total = total + ref[...].astype(jnp.float32)
        heads = jnp.concatenate([query_ref[...], total[:, :k_width]], axis=1)
        turned = rotate(heads, cosine_ref[...], -sine_ref[...])
        out[...] = jnp.concatenate([turned, total[:, k_width:]], axis=1).astype(jnp.bfloat16)

    outs = [((rows, q_width + 2 * k_width), jnp.bfloat16)]
    return kernel_call(body, outs, [grad_query] + list(tables) + list(pair_parts))[0]


def allowed_pairs(position_ref, row_count, key_count, prefix):
    key_offset = lax.broadcasted_iota(jnp.int32, (row_count, key_count), 1) - prefix
    row_index = lax.broadcasted_iota(jnp.int32, (row_count, key_count), 0)
    return (key_offset <= row_index) & (key_offset >= row_index - position_ref[...])


def group_rows(ref, group, size):
    start = group * size * HEAD_DIM
    return jnp.concatenate(
        [ref[:, start + h * HEAD_DIM : start + (h + 1) * HEAD_DIM] for h in range(size)], axis=0
    )


def side_by_side(stacked, row_count):
    return [stacked[h * row_count : (h + 1) * row_count] for h in range(stacked.shape[0] // row_count)]


def attend(query_block, window_blocks, position_block, prefix):
    row_count, q_width = query_block.shape
    k_width = window_blocks[0].shape[1] // 2
    key_count = len(window_blocks) * row_count
    group_size = q_width // k_width

    def body(query_ref, position_ref, *refs):
        *window_refs, out_ref, log_ref = refs
        window = jnp.concatenate([ref[...] for ref in window_refs], axis=0)
        allowed = allowed_pairs(position_ref, row_count, key_count, prefix)
        fill = jnp.where(allowed, 0.0, NEG_FILL)
        fill = jnp.concatenate([fill] * group_size, axis=0)
        columns = []
        for g in range(KV_HEADS):
            span = slice(g * HEAD_DIM, (g + 1) * HEAD_DIM)
            scores = product(group_rows(query_ref, g, group_size), window[:, span], 1, 1)
            scores = jnp.where(fill < 0.0, NEG_FILL, scores * HEAD_DIM ** (-0.5))
            row_max = jnp.max(scores, axis=1, keepdims=True)
            total = jnp.sum(jnp.exp(scores - row_max), axis=1, keepdims=True)
            log_total = row_max + jnp.log(total)
            log_ref[g] = log_total
            prob_low = jnp.exp(scores - log_total).astype(jnp.bfloat16)
            values = window[:, k_width + g * HEAD_DIM : k_width + (g + 1) * HEAD_DIM]
            columns += side_by_side(product(prob_low, values, 1, 0), row_count)
        out_ref[...] = jnp.concatenate(columns, axis=1).astype(jnp.bfloat16)

    outs = [
        ((row_count, q_width), jnp.bfloat16),
        ((KV_HEADS, group_size * row_count, 1), jnp.float32),
    ]
    operands = [query_block, position_block[:, None]] + list(window_blocks)
    return kernel_call(body, outs, operands)


def attend_back(
    query_block, window_blocks, position_block, prefix, log_total, attended_block, grad_block
):
    row_count, q_width = query_block.shape
    k_width = window_blocks[0].shape[1] // 2
    count = len(window_blocks)
    key_count = count * row_count
    group_size = q_width // k_width

    def body(query_ref, position_ref, log_ref, attended_ref, grad_ref, *refs):
        window_refs = refs[:count]
        query_out, *window_outs = refs[count:-7]
        queries, outputs, grads, keys, values, query_grads, pair_grads = refs[-7:]
        allowed = allowed_pairs(position_ref, row_count, key_count, prefix)
        fill = jnp.where(allowed, 0.0, NEG_FILL)
        fill = jnp.concatenate([fill] * group_size, axis=0)
        for g in range(KV_HEADS):
            span = slice(g * HEAD_DIM, (g + 1) * HEAD_DIM)
            value_span = slice(k_width + g * HEAD_DIM, k_width + (g + 1) * HEAD_DIM)
            queries[g] = group_rows(query_ref, g, group_size)
            outputs[g] = group_rows(attended_ref, g, group_size)
            grads[g] = group_rows(grad_ref, g, group_size)
            keys[g] = jnp.concatenate([ref[:, span] for ref in window_refs], axis=0)
            values[g] = jnp.concatenate([ref[:, value_span] for ref in window_refs], axis=0)

        def one_group(g, carry):
            scores = product(queries[g], keys[g], 1, 1)
            scores = jnp.where(fill < 0.0, NEG_FILL, scores * HEAD_DIM ** (-0.5))
            prob_full = jnp.exp(scores - log_ref[g])
            grad_prob = product(grads[g], values[g], 1, 1)
            delta_sum = jnp.sum(
                grads[g].astype(jnp.float32) * outputs[g].astype(jnp.float32),
                axis=1,
                keepdims=True,
            )
            grad_score = (prob_full * (grad_prob - delta_sum) * HEAD_DIM ** (-0.5)).astype(
                jnp.bfloat16
            )
            query_grads[g] = product(grad_score, keys[g], 1, 0)
            pair_grads[0, g] = product(grad_score, queries[g], 0, 0)
            pair_grads[1, g] = product(prob_full.astype(jnp.bfloat16), grads[g], 0, 0)
            return carry

        lax.fori_loop(0, KV_HEADS, one_group, 0)
        columns = []
        for g in range(KV_HEADS):
            columns += side_by_side(query_grads[g], row_count)
        query_out[...] = jnp.concatenate(columns, axis=1)
        for i, out in enumerate(window_outs):
            span = slice(i * row_count, (i + 1) * row_count)
            parts = [pair_grads[p, g, span, :] for p in range(2) for g in range(KV_HEADS)]
            out[...] = jnp.concatenate(parts, axis=1).astype(out.dtype)

    outs = [((row_count, q_width), jnp.float32)]
    outs += [
        ((row_count, 2 * k_width), jnp.float32 if i == count - 1 else LINK) for i in range(count)
    ]
    operands = [query_block, position_block[:, None], log_total, attended_block, grad_block]
    heads = (KV_HEADS, group_size * row_count, HEAD_DIM)
    window_heads = (KV_HEADS, key_count, HEAD_DIM)
    scratch = [pltpu.VMEM(heads, jnp.bfloat16)] * 3 + [pltpu.VMEM(window_heads, jnp.bfloat16)] * 2
    scratch += [pltpu.VMEM(heads, jnp.float32), pltpu.VMEM((2,) + window_heads, jnp.float32)]
    results = kernel_call(body, outs, operands + list(window_blocks), scratch)
    return results[0], results[1:]


def starts_call(body, outs, starts, operands, scratch=()):
    return pl.pallas_call(
        body,
        out_shape=[jax.ShapeDtypeStruct(shape, dtype) for shape, dtype in outs],
        in_specs=[pl.BlockSpec(memory_space=pltpu.SMEM)]
        + [pl.BlockSpec(memory_space=pltpu.VMEM)] * len(operands),
        scratch_shapes=list(scratch),
        compiler_params=pltpu.CompilerParams(vmem_limit_bytes=60 * 1024 * 1024),
    )(starts, *operands)


def arrange_rows(pieces, starts, chunk, order):
    total = sum(piece.shape[0] for piece in pieces)
    width = pieces[0].shape[1]
    if chunk % ROW_TILE:
        stacked = jnp.concatenate(pieces)
        return forward_product(order, stacked).astype(jnp.bfloat16)
    per_piece = pieces[0].shape[0] // chunk

    def body(starts_ref, *refs):
        for j in range(total // chunk):
            at = pl.multiple_of(starts_ref[j], ROW_TILE)
            start = (j % per_piece) * chunk
            refs[-1][pl.ds(at, chunk), :] = refs[j // per_piece][start : start + chunk, :]

    return starts_call(body, [((total, width), jnp.bfloat16)], starts, list(pieces))[0]


def down_products(hidden, grads, starts, chunk, order):
    if chunk % ROW_TILE:
        placed = forward_product(hidden, order).astype(jnp.bfloat16)
        return split_products([placed], jnp.concatenate(grads), hidden.shape[1] // 2)
    half = hidden.shape[1] // 2
    width = grads[0].shape[1]
    count = len(grads)

    def body(starts_ref, *refs):
        hidden_ref = refs[0]
        own, other, total_ref = refs[1 + count :]
        right = jnp.concatenate([refs[1 + i][...] for i in range(count)], axis=0)
        total_ref[...] = product(hidden_ref[...], right, 0, 0)
        for j in range(2 * half // chunk):
            rows = total_ref[pl.ds(pl.multiple_of(starts_ref[j], ROW_TILE), chunk), :]
            target = own if j * chunk < half else other
            start = j * chunk % half
            target[start : start + chunk, :] = rows.astype(target.dtype)

    outs = [((half, width), jnp.float32), ((half, width), LINK)]
    scratch = [pltpu.VMEM((2 * half, width), jnp.float32)]
    return starts_call(body, outs, starts, [hidden] + list(grads), scratch)


def block_products(left_side, down, count):
    rows = left_side.shape[0] // count
    width = down.shape[1]

    def body(left_ref, down_ref, *outs):
        total = product(left_ref[...], down_ref[...], 1, 0)
        for i, out in enumerate(outs):
            out[...] = total[i * rows : (i + 1) * rows].astype(out.dtype)

    outs = [((rows, width), jnp.float32 if i == 0 else LINK) for i in range(count)]
    return kernel_call(body, outs, [left_side, down])


def local(
    hidden_in,
    positions,
    norm1_gain,
    q_weight,
    k_weight,
    v_weight,
    o_weight,
    norm2_gain,
    gate_weight,
    up_weight,
    down_weight,
    cotangent,
):
    tok_rows = hidden_in.shape[0]
    model_width = hidden_in.shape[1]
    device_count = lax.axis_size(AXIS)
    place = lax.axis_index(AXIS)
    member = (place >> TEAM_BITS[0]) & (TEAM - 1)
    outer_index = place >> LOW_BITS
    core = place & 1
    outer_bits = device_count.bit_length() - 1 - LOW_BITS
    top_shift = outer_bits - len(TEAM_BITS)
    window_span = (MAXLEN + tok_rows - 2) // tok_rows
    prefix = window_span * tok_rows
    q_width = q_weight.shape[0] * device_count // model_width
    k_width = k_weight.shape[0] * device_count // model_width
    ff_width = gate_weight.shape[0] * device_count // model_width
    team_width = ff_width // TEAM
    down_rows = ff_width // device_count
    masks = team_masks()

    in_plan = RowPlan(model_width)
    out_plan = RowPlan(q_width)
    paired = len(in_plan.last) > 1

    def both_cores(block):
        return [block, swap(block, 1)] if paired else [block]

    def pair_total(outs):
        return outs[0] + swap(outs[1], 1) if paired else outs[0]

    def distances(plan):
        return [t ^ o for t in plan.team for o in plan.outer_set]

    input_rows = hidden_in.astype(jnp.float32)
    scale_one = norm_scale(input_rows)
    normed_one = (input_rows * scale_one * norm1_gain[None, :]).astype(jnp.bfloat16)
    normed_pair = both_cores(normed_one)

    in_block = in_plan.padded(
        jnp.concatenate([in_plan.whole_rows(w, place) for w in (q_weight, k_weight, v_weight)], 1)
    )
    in_outer = jnp.concatenate(in_plan.outer_pieces(in_block))
    select_in = in_plan.selector(place, distances(in_plan))
    select_out = out_plan.selector(place, distances(out_plan))

    def traded(i):
        outer, mem, c = i >> LOW_BITS, (i >> TEAM_BITS[0]) & (TEAM - 1), i & 1
        inner = outer & ((1 << top_shift) - 1)
        return (((mem << top_shift) | inner) << LOW_BITS) | ((outer >> top_shift) << TEAM_BITS[0]) | c

    trade_route = [(i, traded(i)) for i in range(device_count)]
    chunk_start = []
    for c in range(2):
        for o in in_plan.outer_set:
            o_from = outer_index ^ (o >> LOW_BITS)
            inner = o_from & ((1 << top_shift) - 1)
            chunk = (inner << LOW_BITS) | ((o_from >> top_shift) << TEAM_BITS[0]) | (core ^ c)
            chunk_start.append(chunk * down_rows)
    column = jnp.repeat(jnp.stack(chunk_start), down_rows) + jnp.tile(
        jnp.arange(down_rows, dtype=jnp.int32), len(chunk_start)
    )
    unit_starts = jnp.stack(chunk_start).astype(jnp.int32)
    select_unit = (
        jnp.arange(team_width, dtype=jnp.int32)[:, None] == column[None, :]
    ).astype(jnp.bfloat16)

    def slabs(flat):
        whole = in_plan.whole_rows(flat, place)
        parts = jnp.concatenate(
            [whole[:, t * team_width : (t + 1) * team_width] for t in range(TEAM)]
        )
        return parts.reshape(TEAM, -1, team_width)

    gap = in_plan.pitch - in_plan.rows
    pair_slabs = jnp.pad(
        jnp.concatenate([slabs(gate_weight), slabs(up_weight)], axis=2), ((0, 0), (0, gap), (0, 0))
    )
    member_shift = [m >> TEAM_BITS[0] for m in in_plan.team]
    arrived = [
        swap(pick(pair_slabs, member ^ s), m) if m else pick(pair_slabs, member)
        for s, m in zip(member_shift, in_plan.team)
    ]
    team_index = sum(
        ((place >> (m.bit_length() - 1)) & 1) << i
        for i, m in enumerate(m for m in in_plan.team if m & (m - 1) == 0 and m)
    )
    arrived = jnp.stack(arrived)
    pair_block = jnp.concatenate(
        [pick(arrived, team_index ^ i) for i in range(len(in_plan.team))]
    )
    down_block = lax.ppermute(down_weight.reshape(down_rows, model_width), AXIS, trade_route)
    _, pair_block, down_block, o_flat = tie(in_outer, pair_block, down_block, o_weight)
    weight_in = spread(in_outer, in_plan.team)
    out_pieces = out_plan.outer_pieces(out_plan.padded(out_plan.whole_rows(o_flat, place)))
    pair_outer = in_plan.outer_pieces(pair_block)
    down_outer = in_plan.outer_pieces(down_block)
    out_outer = jnp.concatenate(out_pieces)
    weight_pair = pair_outer + [swap(p, m) for m in in_plan.last[1:] for p in pair_outer]
    ff_distances = [c ^ o ^ t for c in in_plan.last for o in in_plan.outer_set for t in in_plan.team]
    select_ff = in_plan.selector(place & ~in_plan.team[-1], ff_distances)
    weight_down = arrange_rows(
        down_outer + [swap(piece, 1) for piece in down_outer], unit_starts, down_rows, select_unit
    )

    tables = rotary_tables(positions)
    projected_pair, placed_one = pair_project(normed_pair, select_in, weight_in)
    projected_parts = list(projected_pair[:1]) + [swap(part, 1) for part in projected_pair[1:]]
    out_outer, cotangent_late, _ = tie(out_outer, cotangent, projected_parts)
    weight_out = spread(out_outer, out_plan.team)
    query_low, key_value = turn(projected_parts, tables, q_width, k_width)
    pieces = [passed_along(key_value, d) for d in range(window_span, 0, -1)]
    cotangent_blocks = spread(cotangent_late, masks)
    window_blocks = pieces + [key_value]
    attended_low, log_total = attend(query_low, window_blocks, positions, prefix)
    mixed_pair, placed_attended = pair_project(both_cores(attended_low), select_out, weight_out)
    mid_rows = input_rows + pair_total(mixed_pair)
    scale_two = norm_scale(mid_rows)
    normed_two = (mid_rows * scale_two * norm2_gain[None, :]).astype(jnp.bfloat16)

    placed_two = forward_product(normed_two, select_ff).astype(jnp.bfloat16)
    normed_blocks = spread(placed_two, masks)
    hidden_low, grad_low, back_blocks = feed_forward(
        normed_blocks, cotangent_blocks, weight_pair, weight_down
    )
    back_arrived = [swap(block, mask) for block, mask in zip(back_blocks[1:], masks[1:])]
    back_total = back_blocks[0]
    for block in back_arrived:
        back_total = back_total + block.astype(jnp.float32)
    back_high = lax.reduce_precision(back_total, 8, 7)
    grad_normed_two = back_product(back_high.astype(jnp.bfloat16), select_ff) + back_product(
        (back_total - back_high).astype(jnp.bfloat16), select_ff
    )

    pair_rows = placed_two.shape[1] // len(in_plan.last)
    pair_grads = split_products(normed_blocks, grad_low, pair_rows)
    pair_arrived = [swap(g, m) for g, m in zip(pair_grads[1:], in_plan.last[1:])]
    down_grads = down_products(hidden_low, cotangent_blocks, unit_starts, down_rows, select_unit)
    down_arrived = [swap(down_grads[1], 1)]
    outer_group = 1 << len(in_plan.outer[-1])
    pair_own, *pair_blocks = reduce_split(pair_grads[0], pair_arrived, outer_group)
    down_own, *down_blocks = reduce_split(down_grads[0], down_arrived, outer_group)
    pair_sent = in_plan.outer_send(pair_blocks)
    down_sent = in_plan.outer_send(down_blocks)
    grad_mid_norm, grad_gain_two = norm_backward(mid_rows, scale_two, norm2_gain, grad_normed_two)
    grad_mid = cotangent.astype(jnp.float32) + grad_mid_norm
    grad_mid_low = grad_mid.astype(jnp.bfloat16)
    grad_mid_pair = both_cores(grad_mid_low)
    out_grads, attended_pair = pair_back(
        grad_mid_pair, placed_attended, select_out, weight_out
    )
    grad_attended_low = pair_total(attended_pair).astype(jnp.bfloat16)

    out_arrived = [swap(g, m) for g, m in zip(out_grads[1:], out_plan.team[1:])]
    grad_query, grad_windows = attend_back(
        query_low, window_blocks, positions, prefix, log_total, attended_low, grad_attended_low
    )
    pair_parts = [grad_windows[-1]]
    for distance in range(1, window_span + 1):
        pair_parts.append(passed_along(grad_windows[window_span - distance], -distance))
    hidden_late, _ = tie(hidden_low, grad_query)
    out_blocks = block_products(hidden_late, weight_down, TEAM)
    out_swapped = [swap(block, mask) for block, mask in zip(out_blocks[1:], masks[1:])]
    out_total = out_blocks[0]
    for block in out_swapped:
        out_total = out_total + block.astype(jnp.float32)
    block_out = (mid_rows + out_total).astype(jnp.bfloat16)
    grad_projected = turn_back(grad_query, pair_parts, tables)
    grad_projected_pair = both_cores(grad_projected)
    in_grads, normed_grads = pair_back(grad_projected_pair, placed_one, select_in, weight_in)
    in_arrived = [swap(g, m) for g, m in zip(in_grads[1:], in_plan.team[1:])]
    pair_sent, down_sent, _ = tie(pair_sent, down_sent, in_grads[0])
    out_arrived, _ = tie(out_arrived, in_grads[0])
    pair_sum = in_plan.outer_sum(pair_own, pair_sent)
    down_sum = in_plan.outer_sum(down_own, down_sent)
    grad_down = lax.ppermute(down_sum.astype(LINK), AXIS, trade_route).astype(jnp.float32).reshape(-1)
    pair_blocks_t = pair_sum.reshape(len(in_plan.team), in_plan.pitch, 2 * team_width)
    pair_low = pair_blocks_t.astype(LINK)
    returned = [
        swap(pick(pair_low, team_index ^ i), m) if m else pick(pair_low, team_index)
        for i, m in enumerate(in_plan.team)
    ]
    back_stack = jnp.stack(returned)[:, : in_plan.rows]
    natural = (back_stack[:, :, :team_width], back_stack[:, :, team_width:])

    def owned(grad_slabs):
        columns = []
        for t in range(TEAM):
            column_part = jnp.zeros_like(grad_slabs[0])
            for i, s in enumerate(member_shift):
                column_part = jnp.where((member ^ s) == t, grad_slabs[i], column_part)
            columns.append(column_part)
        return in_plan.own_share(
            jnp.concatenate(columns, axis=1).astype(jnp.float32), place
        )

    grad_gate = owned(natural[0])
    grad_up = owned(natural[1])

    def team_share(plan, own, arrived_blocks):
        own, *blocks = reduce_split(own, arrived_blocks, 1 << len(plan.outer[-1]))
        return own, blocks

    out_own, out_split = team_share(out_plan, out_grads[0], out_arrived)
    out_sent = out_plan.outer_send(out_split)
    in_own, in_split = team_share(in_plan, in_grads[0], in_arrived)
    in_sent = in_plan.outer_send(in_split)
    out_share = out_plan.outer_sum(out_own, out_sent)[: out_plan.rows]
    grad_out = out_plan.own_share(out_share, place)
    if len(in_plan.outer) == 1:
        in_shares = sum_columns(in_own, in_sent, in_plan.rows, (q_width, k_width, k_width))
    else:
        in_share = in_plan.outer_sum(in_own, in_sent)[: in_plan.rows]
        in_shares = jnp.split(in_share, [q_width, q_width + k_width], axis=1)
    grad_query_weight, grad_key_weight, grad_value_weight = (
        in_plan.own_share(share, place) for share in in_shares
    )
    grad_normed_one = pair_total(normed_grads)
    grad_in_norm, grad_gain_one = norm_backward(input_rows, scale_one, norm1_gain, grad_normed_one)
    grad_in = (grad_mid + grad_in_norm).astype(jnp.bfloat16)
    gains = jnp.stack([grad_gain_one, grad_gain_two])
    for bit in range(device_count.bit_length() - 1):
        if bit < 1:
            gains = reduce_split(gains, [swap(gains, 1 << bit)], 1)[0]
        else:
            gains = gains + swap(gains, 1 << bit)
    return (
        block_out,
        grad_in,
        gains[0],
        grad_query_weight,
        grad_key_weight,
        grad_value_weight,
        grad_out,
        gains[1],
        grad_gate,
        grad_up,
        grad_down,
    )


def solution(mesh):
    placed = (
        P("fsdp", None),
        P("fsdp"),
        P(),
        P("fsdp"),
        P("fsdp"),
        P("fsdp"),
        P("fsdp"),
        P(),
        P("fsdp"),
        P("fsdp"),
        P("fsdp"),
        P("fsdp", None),
    )
    return jax.shard_map(
        local,
        mesh=mesh,
        in_specs=placed,
        out_specs=(
            P("fsdp", None),
            P("fsdp", None),
            P(),
            P("fsdp"),
            P("fsdp"),
            P("fsdp"),
            P("fsdp"),
            P(),
            P("fsdp"),
            P("fsdp"),
            P("fsdp"),
        ),
        check_vma=False,
    )
```
